32 devices in a mesh: rows: 8 (over y, x, core), agg: 4 (over z).
Axes of the slice: x: 2, y: 2, z: 4, core: 2. Of those that a mesh axis runs over, the one named last changes fastest.
Arguments:
- load_rhs: bfloat16 [2048, 128, 128], P(('rows', 'agg')), may hold values from -6 to 6
- blocks: bfloat16 [2048, 8, 128, 128], P(('rows', 'agg'))
- columns: int32 [2048, 8], P(('rows', 'agg')), may hold values from 0 to 2047, as said below
- counts: int32 [2048], P(('rows', 'agg')), may hold values from 3 to 8, as said below
- smoother: bfloat16 [2048, 128, 128], P(('rows', 'agg'))
- agg_sizes: int32 [8, 32], P('rows'), may hold values from 1 to 24, 256 in all within a row
- coarse_inv: bfloat16 [256, 128, 128], P(('rows', 'agg'))
Outputs:
- corrected: float32 [2048, 128, 128], P(('rows', 'agg'))
The draws below stay inside these ranges and needn't reach their ends.
Inputs may be any that keep to these rules, and one draw needn't show every extreme that they name: columns[i, k] lies within 16 of i; slot 0 is i, slot 1 is min(i + 16, 2047), slot 2 is max(i - 16, 0). `counts`: slots 0 to 2 are always live; the first block row of each device has all 8 live. `agg_sizes`: each row sums to 256.
All inputs are finite; a program needn't handle non-finite values.
Results may differ from the reference program's by a relative error of at most 0.0044.
Values may be sent and summed in bfloat16 or wider, within the bound.
No kernel may reach another device: no remote copies, remote signals or barrier semaphores. Data moves between devices by JAX's collectives and lax.ppermute only.
A program may use at most 192 MiB of HBM per device.

```python
import math
import jax
import jax.numpy as jnp
import numpy as np
from jax import lax

BS = 128
NRHS = 128
K = 8
MEAN_AGG = 8
R_DEV = 64
HALO = 16
GROUP_AGGS = 32
NB = 2048
NAGG = 256
N_ROWS = 8
N_AGG = 4


def noise_field(key, shape):
    return jax.random.normal(key, shape, jnp.float32)


def identity_like(shape):
    row_ids = jax.lax.broadcasted_iota(jnp.int32, shape, len(shape) - 2)
    col_ids = jax.lax.broadcasted_iota(jnp.int32, shape, len(shape) - 1)
    return (row_ids == col_ids).astype(jnp.float32)


def draw_blocks(key, part):
    shape = (NB, K, BS, BS)
    slot_ids = jax.lax.broadcasted_iota(jnp.int32, shape, 1)
    diagonal = identity_like(shape) * (slot_ids == 0).astype(jnp.float32) * 2.0
    return (diagonal + noise_field(jax.random.fold_in(key, 11), shape) / BS ** 0.5).astype(jnp.bfloat16)


def draw_columns(key, part):
    row_ids = jnp.arange(NB, dtype=jnp.int32)[:, None]
    offsets = jax.random.randint(jax.random.fold_in(key, 21), (NB, K), -HALO, HALO + 1).astype(jnp.int32)
    slot_ids = jnp.arange(K, dtype=jnp.int32)[None, :]
    offsets = jnp.where(slot_ids == 0, 0, jnp.where(slot_ids == 1, HALO, jnp.where(slot_ids == 2, -HALO, offsets)))
    return jnp.clip(row_ids + offsets, 0, NB - 1).astype(jnp.int32)


def draw_counts(key, part):
    drawn = jax.random.randint(jax.random.fold_in(key, 31), (NB,), 3, K + 1).astype(jnp.int32)
    row_ids = jnp.arange(NB, dtype=jnp.int32)
    return jnp.where(row_ids % R_DEV == 0, K, drawn).astype(jnp.int32)


def draw_smoother(key, part):
    shape = (NB, BS, BS)
    return (0.25 * (identity_like(shape) + 0.5 * noise_field(jax.random.fold_in(key, 41), shape) / BS ** 0.5)).astype(jnp.bfloat16)


def draw_coarse_inv(key, part):
    shape = (NAGG, BS, BS)
    return (0.05 * (identity_like(shape) + 0.5 * noise_field(jax.random.fold_in(key, 51), shape) / BS ** 0.5)).astype(jnp.bfloat16)


def level_of(stream_key, dims, pieces, low, largest):
    level = 1.0
    for axis_at, shards_of in pieces:
        heights = jax.random.uniform(jax.random.fold_in(jax.random.fold_in(stream_key, 6), axis_at), (shards_of,), jnp.float32, low / len(pieces), largest / len(pieces))
        level = level * jnp.repeat(jnp.exp(heights), dims[axis_at] // shards_of).reshape((-1,) + (1,) * (len(dims) - 1 - axis_at))
    return level


def profile(count, total, most, skew):
    loads = [(1 << 20) // math.isqrt(rank ** skew) + 1 for rank in range(2, count + 1)]
    rest, holding = total - most - (count - 1), [1] * (count - 1)
    while rest > 0:
        movable = [i for i in range(count - 1) if holding[i] < most]
        whole, budget = sum([loads[i] for i in movable]), rest
        for i in movable:
            addition = min(most - holding[i], max(1, budget * loads[i] // whole), rest)
            holding[i] = holding[i] + addition
            rest = rest - addition
    return np.array([most] + holding)


def ragged(key, amount, total, reach, skew):
    if amount == 2:
        one = jax.random.randint(key, (), max(1, total - reach), min(reach, total - 1) + 1)
        return jnp.stack([one, total - one])
    lengths = jnp.asarray(profile(amount, total, reach, skew), jnp.int32)
    couples = (amount - 1) // 2
    source_of, taker = lengths[1:1 + 2 * couples:2], lengths[2:2 + 2 * couples:2]
    slack = jnp.minimum(source_of - 1, reach - taker)
    passed = jax.random.randint(jax.random.fold_in(key, 1), (couples,), 0, 1 << 20) % (slack + 1)
    lengths = lengths.at[1:1 + 2 * couples:2].set(source_of - passed).at[2:2 + 2 * couples:2].set(taker + passed)
    return lengths[jax.random.permutation(jax.random.fold_in(key, 2), amount)]


def centred(stream_key, dims, deviation, bound, shards=(), kind=jnp.bfloat16):
    entries = deviation * jax.random.normal(stream_key, dims, jnp.float32)
    if shards:
        entries = entries * level_of(stream_key, dims, shards, -0.22, 0.18)
    return jnp.clip(entries, -bound, bound).astype(kind)


def setup_inputs(seed: int = 0) -> dict:
    arg_keys = jax.random.split(jax.random.key(seed), 8)
    return {
        "load_rhs": centred(arg_keys[0], (NB, BS, NRHS), 1.0, 6.0, ((0, 32),)),
        "blocks": draw_blocks(jax.random.fold_in(arg_keys[7], 71), 0),
        "columns": draw_columns(jax.random.fold_in(arg_keys[7], 71), 0),
        "counts": draw_counts(jax.random.fold_in(arg_keys[7], 71), 0),
        "smoother": draw_smoother(jax.random.fold_in(arg_keys[7], 71), 0),
        "agg_sizes": jax.vmap(lambda own: ragged(own, GROUP_AGGS, R_DEV * N_AGG, 3 * MEAN_AGG, 2))(jax.random.split(arg_keys[5], N_ROWS)).reshape((N_ROWS, GROUP_AGGS)).astype(jnp.int32),
        "coarse_inv": draw_coarse_inv(jax.random.fold_in(arg_keys[7], 71), 0),
    }


relax_fine = 0.8
relax_coarse = 1.0


def apply_diag(inverse, vector):
    return jnp.einsum('rij,rjn->rin', inverse.astype(jnp.float32), vector.astype(jnp.float32))


def reference(load_rhs, blocks, columns, counts, smoother, agg_sizes, coarse_inv):
    total = load_rhs.shape[0]
    dev_count = N_ROWS * N_AGG
    group_aggs = agg_sizes.shape[1]
    slot_range = jnp.arange(K, dtype=jnp.int32)
    live_mask = (slot_range[None, :] < counts[:, None]).astype(jnp.float32)

    def apply_blocks(vector):
        def per_device(items):
            block_part, col_part, mask_part = items
            gathered = vector[col_part].astype(jnp.float32) * mask_part[:, :, None, None]
            return jnp.einsum('rkij,rkjn->rin', block_part.astype(jnp.float32), gathered)

        result = lax.map(per_device, (blocks.reshape(dev_count, R_DEV, K, BS, BS),
                                      columns.reshape(dev_count, R_DEV, K),
                                      live_mask.reshape(dev_count, R_DEV, K)))
        return result.reshape(total, BS, NRHS)

    rhs_full = load_rhs.astype(jnp.float32)
    smooth_one = relax_fine * apply_diag(smoother, load_rhs)
    resid_one = (rhs_full - apply_blocks(smooth_one.astype(jnp.bfloat16))).astype(jnp.bfloat16)
    smooth_two = smooth_one + relax_fine * apply_diag(smoother, resid_one)
    resid_two = (rhs_full - apply_blocks(smooth_two.astype(jnp.bfloat16))).astype(jnp.bfloat16)

    def per_group(items):
        resid, sizes, inverse = items
        agg_ends = jnp.cumsum(sizes)
        fine_index = jnp.arange(N_AGG * R_DEV, dtype=jnp.int32)
        agg_index = jnp.sum((agg_ends[None, :] <= fine_index[:, None]).astype(jnp.int32), axis=1)
        member = (agg_index[:, None] == jnp.arange(group_aggs, dtype=jnp.int32)[None, :]).astype(jnp.float32)
        member_dev = member.reshape(N_AGG, R_DEV, group_aggs)
        resid_dev = resid.reshape(N_AGG, R_DEV, BS, NRHS).astype(jnp.float32)
        partial_value = jnp.einsum('qra,qrin->qain', member_dev, resid_dev).astype(jnp.bfloat16).astype(jnp.float32)
        coarse_res = jnp.sum(partial_value, axis=0).astype(jnp.bfloat16)
        coarse_fix = (relax_coarse * apply_diag(inverse, coarse_res)).astype(jnp.bfloat16)
        return jnp.einsum('ra,ain->rin', member, coarse_fix.astype(jnp.float32))

    prolonged = lax.map(per_group, (resid_two.reshape(N_ROWS, N_AGG * R_DEV, BS, NRHS),
                                    agg_sizes,
                                    coarse_inv.reshape(N_ROWS, group_aggs, BS, BS)))
    return smooth_two + prolonged.reshape(total, BS, NRHS)
```

```python
import jax
import jax.numpy as jnp
from jax import lax
from jax.experimental import pallas as pl
from jax.experimental.pallas import tpu as pltpu
from jax.sharding import PartitionSpec as P

HALO = 16
RB = 4

relax_fine = 0.8
relax_coarse = 1.0

AXES = ("rows", "agg")
F32 = jnp.float32
BF16 = jnp.bfloat16
VMEM_BYTES = 56 * 1024 * 1024


def mm(a, b):
    return jnp.dot(a, b, preferred_element_type=F32)


def params():
    return pltpu.CompilerParams(
        vmem_limit_bytes=VMEM_BYTES, dimension_semantics=("arbitrary",)
    )


def cost(flops, nbytes):
    return pl.CostEstimate(flops=flops, bytes_accessed=nbytes, transcendentals=0)


def smem():
    return pl.BlockSpec(memory_space=pltpu.SMEM)


def const_spec(shape):
    return pl.BlockSpec(
        shape, lambda s: (0,) * len(shape), pipeline_mode=pl.Buffered(1)
    )


def sds(rows, bs, n, dtype):
    return jax.ShapeDtypeStruct((rows, bs, n), dtype)


class Plan:
    def __init__(self, rows, slots, bs, n):
        self.R, self.K, self.BS, self.N = rows, slots, bs, n
        self.H = HALO
        self.I = rows - 2 * HALO
        self.nlo = HALO // RB
        self.nin = self.I // RB
        self.steps = rows // RB

    def edge_step(self, s):
        return jnp.where(s < self.nlo, s, s + self.nin)

    def edge_out(self, s):
        return jnp.where(
            s < self.nlo, s, jnp.where(s < self.nlo + self.nin, self.nlo - 1, s - self.nin)
        )

    def inner_out(self, s):
        return jnp.clip(s - self.nlo, 0, self.nin - 1)


def edge_smooth(p, rhs, smoother):
    def kernel(b_ref, s_ref, lo_ref, hi_ref):
        s = pl.program_id(0)

        def do(out):
            for r in range(RB):
                out[r] = (relax_fine * mm(s_ref[r], b_ref[r])).astype(BF16)

        pl.when(s < p.nlo)(lambda: do(lo_ref))
        pl.when(s >= p.nlo)(lambda: do(hi_ref))

    blk = lambda w: pl.BlockSpec((RB, p.BS, w), lambda s: (p.edge_step(s), 0, 0))
    lo = pl.BlockSpec((RB, p.BS, p.N), lambda s: (jnp.minimum(s, p.nlo - 1), 0, 0))
    hi = pl.BlockSpec((RB, p.BS, p.N), lambda s: (jnp.maximum(s - p.nlo, 0), 0, 0))
    out = sds(p.H, p.BS, p.N, BF16)
    return pl.pallas_call(
        kernel,
        grid=(2 * p.nlo,),
        in_specs=[blk(p.N), blk(p.BS)],
        out_specs=[lo, hi],
        out_shape=[out, out],
        compiler_params=params(),
        cost_estimate=cost(4 * p.H * p.BS * p.BS * p.N, 6 * p.H * p.BS * p.N),
        name="edge_smooth",
    )(rhs, smoother)


def row_product(p, blk_ref, r, ext, cols, at):
    lhs = jnp.concatenate([blk_ref[r, k] for k in range(p.K)], axis=1)
    rhs = jnp.concatenate([ext[cols[at + k]] for k in range(p.K)], axis=0)
    return mm(lhs, rhs)


def inner_first(p, lcol, rhs, smoother, blocks):
    def kernel(lcol_ref, b_ref, s_ref, blk_ref, s2_ref, s2b_ref, acc_ref, ext, s1):
        s = pl.program_id(0)

        @pl.when(s == 0)
        def _():
            ext[p.R] = jnp.zeros((p.BS, p.N), BF16)

            def one(r, c):
                v = relax_fine * mm(s_ref[r], b_ref[r])
                s1[r] = v
                ext[r] = v.astype(BF16)
                return c

            lax.fori_loop(0, p.R, one, 0, unroll=4)

        is_edge = jnp.logical_or(s < p.nlo, s >= p.nlo + p.nin)

        @pl.when(is_edge)
        def _():
            for r in range(RB):
                i = s * RB + r
                acc_ref[r] = b_ref[i].astype(F32) - row_product(p, blk_ref, r, ext, lcol_ref, i * p.K)
                s2_ref[r] = s1[i]

        @pl.when(jnp.logical_not(is_edge))
        def _():
            for r in range(RB):
                i = s * RB + r
                res = b_ref[i].astype(F32) - row_product(p, blk_ref, r, ext, lcol_ref, i * p.K)
                v = s1[i] + relax_fine * mm(s_ref[i], res.astype(BF16))
                s2_ref[r] = v
                s2b_ref[r] = v.astype(BF16)

    return pl.pallas_call(
        kernel,
        grid=(p.steps,),
        in_specs=[
            smem(),
            const_spec((p.R, p.BS, p.N)),
            const_spec((p.R, p.BS, p.BS)),
            pl.BlockSpec((RB, p.K, p.BS, p.BS), lambda s: (s, 0, 0, 0)),
        ],
        out_specs=[
            pl.BlockSpec((RB, p.BS, p.N), lambda s: (s, 0, 0)),
            pl.BlockSpec((RB, p.BS, p.N), lambda s: (p.inner_out(s), 0, 0)),
            pl.BlockSpec((RB, p.BS, p.N), lambda s: (p.edge_out(s), 0, 0)),
        ],
        out_shape=[
            sds(p.R, p.BS, p.N, F32),
            sds(p.I, p.BS, p.N, BF16),
            sds(2 * p.H, p.BS, p.N, F32),
        ],
        scratch_shapes=[
            pltpu.VMEM((p.R + 1, p.BS, p.N), BF16),
            pltpu.VMEM((p.R, p.BS, p.N), F32),
        ],
        compiler_params=params(),
        cost_estimate=cost(2 * p.R * p.K * p.BS * p.BS * p.N, 2 * p.R * p.K * p.BS * p.BS),
        name="inner_first",
    )(lcol, rhs, smoother, blocks)


def edge_residual(p, hslot, hcol, hn, i, r, blk_ref, halo, acc_ref):
    at = i * p.K

    def pair(j):
        lhs = jnp.concatenate([blk_ref[r, hslot[at + j]], blk_ref[r, hslot[at + j + 1]]], axis=1)
        rhs = jnp.concatenate([halo[hcol[at + j]], halo[hcol[at + j + 1]]], axis=0)
        return mm(lhs, rhs)

    acc_ref[r] = acc_ref[r] - pair(0)

    @pl.when(hn[i] > 2)
    def _():
        rest = pair(2)
        for j in range(4, p.K, 2):
            rest = rest + pair(j)
        acc_ref[r] = acc_ref[r] - rest

    return acc_ref[r].astype(BF16)


def fill_halo(p, s, before_ref, after_ref, halo):
    @pl.when(s == 0)
    def _():
        halo[:p.H] = before_ref[...]
        halo[p.H:2 * p.H] = after_ref[...]
        halo[2 * p.H] = jnp.zeros((p.BS, p.N), BF16)


def edge_second(p, hslot, hcol, hn, before, after, acc, smoother, blocks, s2):
    def kernel(hs, hc, hn_ref, bef, aft, acc_in, s_ref, blk_ref, s2_in, s2_out, lo_ref, hi_ref, halo, work):
        s = pl.program_id(0)
        fill_halo(p, s, bef, aft, halo)
        work[...] = acc_in[...]

        def do(out):
            for r in range(RB):
                i = p.edge_step(s) * RB + r
                res = edge_residual(p, hs, hc, hn_ref, i, r, blk_ref, halo, work)
                v = s2_in[r] + relax_fine * mm(s_ref[r], res)
                s2_out[r] = v
                out[r] = v.astype(BF16)

        pl.when(s < p.nlo)(lambda: do(lo_ref))
        pl.when(s >= p.nlo)(lambda: do(hi_ref))

    blk = lambda w: pl.BlockSpec((RB, p.BS, w), lambda s: (p.edge_step(s), 0, 0))
    lo = pl.BlockSpec((RB, p.BS, p.N), lambda s: (jnp.minimum(s, p.nlo - 1), 0, 0))
    hi = pl.BlockSpec((RB, p.BS, p.N), lambda s: (jnp.maximum(s - p.nlo, 0), 0, 0))
    out = sds(p.H, p.BS, p.N, BF16)
    return pl.pallas_call(
        kernel,
        grid=(2 * p.nlo,),
        in_specs=[
            smem(),
            smem(),
            smem(),
            const_spec((p.H, p.BS, p.N)),
            const_spec((p.H, p.BS, p.N)),
            pl.BlockSpec((RB, p.BS, p.N), lambda s: (s, 0, 0)),
            blk(p.BS),
            pl.BlockSpec((RB, p.K, p.BS, p.BS), lambda s: (p.edge_step(s), 0, 0, 0)),
            blk(p.N),
        ],
        out_specs=[blk(p.N), lo, hi],
        out_shape=[sds(p.R, p.BS, p.N, F32), out, out],
        input_output_aliases={8: 0},
        scratch_shapes=[
            pltpu.VMEM((2 * p.H + 1, p.BS, p.N), BF16),
            pltpu.VMEM((RB, p.BS, p.N), F32),
        ],
        compiler_params=params(),
        cost_estimate=cost(8 * p.H * p.BS * p.BS * p.N, 4 * p.H * p.K * p.BS * p.BS),
        name="edge_second",
    )(hslot, hcol, hn, before, after, acc, smoother, blocks, s2)


def inner_residual(p, lcol, rhs, blocks, lo, inner, hi):
    def kernel(lcol_ref, lo_ref, in_ref, hi_ref, b_ref, blk_ref, r2_ref, acc_ref, ext):
        s = pl.program_id(0)

        @pl.when(s == 0)
        def _():
            ext[:p.H] = lo_ref[...]
            ext[p.H:p.R - p.H] = in_ref[...]
            ext[p.R - p.H:p.R] = hi_ref[...]
            ext[p.R] = jnp.zeros((p.BS, p.N), BF16)

        is_edge = jnp.logical_or(s < p.nlo, s >= p.nlo + p.nin)

        def do(out):
            for r in range(RB):
                i = s * RB + r
                res = b_ref[r].astype(F32) - row_product(p, blk_ref, r, ext, lcol_ref, i * p.K)
                out[r] = res.astype(out.dtype)

        pl.when(is_edge)(lambda: do(acc_ref))
        pl.when(jnp.logical_not(is_edge))(lambda: do(r2_ref))

    return pl.pallas_call(
        kernel,
        grid=(p.steps,),
        in_specs=[
            smem(),
            const_spec((p.H, p.BS, p.N)),
            const_spec((p.I, p.BS, p.N)),
            const_spec((p.H, p.BS, p.N)),
            pl.BlockSpec((RB, p.BS, p.N), lambda s: (s, 0, 0)),
            pl.BlockSpec((RB, p.K, p.BS, p.BS), lambda s: (s, 0, 0, 0)),
        ],
        out_specs=[
            pl.BlockSpec((RB, p.BS, p.N), lambda s: (p.inner_out(s), 0, 0)),
            pl.BlockSpec((RB, p.BS, p.N), lambda s: (p.edge_out(s), 0, 0)),
        ],
        out_shape=[sds(p.I, p.BS, p.N, BF16), sds(2 * p.H, p.BS, p.N, F32)],
        scratch_shapes=[pltpu.VMEM((p.R + 1, p.BS, p.N), BF16)],
        compiler_params=params(),
        cost_estimate=cost(2 * p.R * p.K * p.BS * p.BS * p.N, 2 * p.R * p.K * p.BS * p.BS),
        name="inner_residual",
    )(lcol, lo, inner, hi, rhs, blocks)


def aggregate_sum(resid, first, last, shape):
    return lax.fori_loop(first, last, lambda r, t: t + resid[r].astype(F32), jnp.zeros(shape, F32))


def edge_final(p, hslot, hcol, hn, ends, before, after, acc, blocks, inner):
    last = 2 * p.nlo - 1

    def kernel(hs, hc, hn_ref, ends_ref, bef, aft, acc_in, blk_ref, in_ref, r2_ref, pf_ref, pl_ref, halo, work):
        s = pl.program_id(0)
        fill_halo(p, s, bef, aft, halo)
        work[...] = acc_in[...]

        @pl.when(s == 0)
        def _():
            r2_ref[p.H:p.R - p.H] = in_ref[...]

        for r in range(RB):
            i = p.edge_step(s) * RB + r
            r2_ref[i] = edge_residual(p, hs, hc, hn_ref, i, r, blk_ref, halo, work)

        @pl.when(s == last)
        def _():
            pf_ref[...] = aggregate_sum(r2_ref, 0, ends_ref[0], (p.BS, p.N)).astype(BF16)
            pl_ref[...] = aggregate_sum(r2_ref, ends_ref[1], p.R, (p.BS, p.N)).astype(BF16)

    return pl.pallas_call(
        kernel,
        grid=(2 * p.nlo,),
        in_specs=[
            smem(),
            smem(),
            smem(),
            smem(),
            const_spec((p.H, p.BS, p.N)),
            const_spec((p.H, p.BS, p.N)),
            pl.BlockSpec((RB, p.BS, p.N), lambda s: (s, 0, 0)),
            pl.BlockSpec((RB, p.K, p.BS, p.BS), lambda s: (p.edge_step(s), 0, 0, 0)),
            const_spec((p.I, p.BS, p.N)),
        ],
        out_specs=[
            const_spec((p.R, p.BS, p.N)),
            const_spec((p.BS, p.N)),
            const_spec((p.BS, p.N)),
        ],
        out_shape=[
            sds(p.R, p.BS, p.N, BF16),
            jax.ShapeDtypeStruct((p.BS, p.N), BF16),
            jax.ShapeDtypeStruct((p.BS, p.N), BF16),
        ],
        scratch_shapes=[
            pltpu.VMEM((2 * p.H + 1, p.BS, p.N), BF16),
            pltpu.VMEM((RB, p.BS, p.N), F32),
        ],
        compiler_params=params(),
        cost_estimate=cost(4 * p.H * p.BS * p.BS * p.N, 4 * p.H * p.K * p.BS * p.BS),
        name="edge_final",
    )(hslot, hcol, hn, ends, before, after, acc, blocks, inner)


def coarse(p, bounds, joins, own, r2, s2, from_before, from_after, inverses):
    aggs = bounds.shape[0] - 1
    group = len(inverses)
    share = aggs // group

    def kernel(bd, jn, ow, bef, aft, r2_ref, s2_ref, *rest):
        inv_refs, out_ref, inv, sems = rest[:group], rest[group], rest[group + 1], rest[group + 2]
        copies = []
        for t in range(group):
            place = lax.rem(ow[0] - t + group, group) * share
            copies.append(pltpu.make_async_copy(inv_refs[t], inv.at[pl.ds(place, share)], sems.at[t]))
            copies[-1].start()
        for c in copies:
            c.wait()

        def one(a, c):
            first, last = bd[a], bd[a + 1]

            @pl.when(first < last)
            def _():
                part = aggregate_sum(r2_ref, first, last, (p.BS, p.N)).astype(BF16).astype(F32)
                left = jnp.where(jnp.logical_and(first == 0, jn[0] > 0), bef[...].astype(F32), 0.0)
                right = jnp.where(jnp.logical_and(last == p.R, jn[1] > 0), aft[...].astype(F32), 0.0)
                res = (left + part + right).astype(BF16)
                fix = (relax_coarse * mm(inv[a], res)).astype(BF16).astype(F32)

                def add(r, c):
                    out_ref[r] = s2_ref[r] + fix
                    return c

                lax.fori_loop(first, last, add, 0)

            return c

        lax.fori_loop(0, aggs, one, 0)

    vm = pl.BlockSpec(memory_space=pltpu.VMEM)
    anyspec = pl.BlockSpec(memory_space=pl.ANY)
    return pl.pallas_call(
        kernel,
        in_specs=[smem(), smem(), smem(), vm, vm, vm, vm] + [anyspec] * group,
        out_specs=vm,
        out_shape=sds(p.R, p.BS, p.N, F32),
        scratch_shapes=[
            pltpu.VMEM((aggs, p.BS, p.BS), BF16),
            pltpu.SemaphoreType.DMA((group,)),
        ],
        compiler_params=pltpu.CompilerParams(vmem_limit_bytes=VMEM_BYTES),
        cost_estimate=cost(2 * aggs * p.BS * p.BS * p.N, 10 * p.R * p.BS * p.N),
        name="coarse",
    )(bounds, joins, own, from_before, from_after, r2, s2, *inverses)


def shift(value, axis, up):
    size = lax.axis_size(axis)
    pairs = [(i, i + 1) for i in range(size - 1)]
    return lax.ppermute(value, axis, pairs if up else [(j, i) for i, j in pairs])


def body(load_rhs, blocks, columns, counts, smoother, agg_sizes, coarse_inv):
    rows, bs, n = load_rhs.shape
    slots = blocks.shape[1]
    p = Plan(rows, slots, bs, n)
    aggs = agg_sizes.shape[1]
    group = lax.axis_size("agg")

    start = lax.axis_index(AXES) * rows
    local = columns - start
    ks = jnp.arange(slots, dtype=jnp.int32)
    live = ks[None, :] < counts[:, None]
    inside = jnp.logical_and(local >= 0, local < rows)
    lcol = jnp.where(jnp.logical_and(live, inside), local, rows).reshape(-1)
    outside = jnp.logical_and(live, jnp.logical_not(inside))
    place = jnp.where(local < 0, local + HALO, local - rows + HALO)
    rank = jnp.sum(
        jnp.where(jnp.logical_and(outside[:, None, :], ks[None, None, :] < ks[None, :, None]), 1, 0), axis=2
    )
    taken = jnp.logical_and(outside[:, None, :], rank[:, None, :] == ks[None, :, None])
    hslot = jnp.sum(jnp.where(taken, ks[None, None, :], 0), axis=2).reshape(-1)
    hcol = (2 * HALO + jnp.sum(jnp.where(taken, place[:, None, :] - 2 * HALO, 0), axis=2)).reshape(-1)
    hn = jnp.sum(outside.astype(jnp.int32), axis=1)

    here = lax.axis_index("agg")
    a_ids = jnp.arange(aggs + 1, dtype=jnp.int32)
    ends = jnp.sum(jnp.where(a_ids[None, :aggs] < a_ids[:, None], agg_sizes[0][None, :], 0), axis=1)
    rel = ends - here * rows
    bounds = jnp.clip(rel, 0, rows)
    first_end = jnp.min(jnp.where(rel > 0, rel, rows * group))
    last_begin = jnp.max(jnp.where(rel < rows, rel, -rows * group))
    trims = jnp.stack([jnp.clip(first_end, 0, rows), jnp.clip(last_begin, 0, rows)])
    joins = jnp.stack(
        [
            jnp.logical_not(jnp.any(rel == 0)).astype(jnp.int32),
            jnp.logical_not(jnp.any(rel == rows)).astype(jnp.int32),
        ]
    )
    own = here[None].astype(jnp.int32)

    lo1, hi1 = edge_smooth(p, load_rhs, smoother)
    before1, after1 = shift(hi1, AXES, True), shift(lo1, AXES, False)
    s2, s2_inner, acc1 = inner_first(p, lcol, load_rhs, smoother, blocks)
    s2, lo2, hi2 = edge_second(p, hslot, hcol, hn, before1, after1, acc1, smoother, blocks, s2)
    before2, after2 = shift(hi2, AXES, True), shift(lo2, AXES, False)
    r2_inner, acc2 = inner_residual(p, lcol, load_rhs, blocks, lo2, s2_inner, hi2)

    inverses = [coarse_inv]
    for t in range(1, group):
        inverses.append(
            lax.ppermute(coarse_inv, "agg", [(i, (i + t) % group) for i in range(group)])
        )

    r2, part_first, part_last = edge_final(p, hslot, hcol, hn, trims, before2, after2, acc2, blocks, r2_inner)
    from_before, from_after = shift(part_last, "agg", True), shift(part_first, "agg", False)
    return coarse(p, bounds, joins, own, r2, s2, from_before, from_after, inverses)


def solution(mesh):
    placed = (
        P(AXES, None, None),
        P(AXES, None, None, None),
        P(AXES, None),
        P(AXES),
        P(AXES, None, None),
        P("rows", None),
        P(AXES, None, None),
    )
    return jax.shard_map(
        body, mesh=mesh, in_specs=placed, out_specs=P(AXES, None, None), check_vma=False
    )
```

```python
import jax
import jax.numpy as jnp
from jax import lax
from jax.experimental import pallas as pl
from jax.experimental.pallas import tpu as pltpu
from jax.sharding import PartitionSpec as P

HALO = 16

relax_fine = 0.8
relax_coarse = 1.0

AXES = ("rows", "agg")
F32 = jnp.float32
BF16 = jnp.bfloat16
I32 = jnp.int32
MIB = 1024 * 1024
WEIGHT = 32

SMEM = pl.BlockSpec(memory_space=pltpu.SMEM)
VM = pl.BlockSpec(memory_space=pltpu.VMEM)
ANY = pl.BlockSpec(memory_space=pl.ANY)
HBM = pl.BlockSpec(memory_space=pltpu.HBM)


def mm(a, b):
    return jnp.dot(a, b, preferred_element_type=F32)


def cost(flops, nbytes):
    return pl.CostEstimate(flops=WEIGHT * flops, bytes_accessed=nbytes, transcendentals=0)


def params(mib):
    return pltpu.CompilerParams(vmem_limit_bytes=mib * MIB)


def near(x):
    return pltpu.with_memory_space_constraint(x, pltpu.VMEM)


def far(x):
    return pltpu.with_memory_space_constraint(x, pltpu.HBM)


class Sizes:
    def __init__(self, rows, slots, bs, n, aggs, group):
        self.R, self.K, self.BS, self.N, self.A, self.G = rows, slots, bs, n, aggs, group
        self.H = HALO


def edge_smooth(p, rhs, smoother):
    step = 8
    starts = [0, step, p.R - p.H, p.R - p.H + step]

    def kernel(b_hbm, s_hbm, lo_ref, hi_ref, b, s, sems):
        copies = []
        for c, at in enumerate(starts):
            copies.append(pltpu.make_async_copy(b_hbm.at[pl.ds(at, step)], b.at[c], sems.at[0, c]))
            copies.append(pltpu.make_async_copy(s_hbm.at[pl.ds(at, step)], s.at[c], sems.at[1, c]))
        for c in copies:
            c.start()
        for c in range(len(starts)):
            copies[2 * c].wait()
            copies[2 * c + 1].wait()
            out = lo_ref if c < 2 else hi_ref
            for r in range(step):
                out[(c % 2) * step + r] = (relax_fine * mm(s[c, r], b[c, r])).astype(BF16)

    out = jax.ShapeDtypeStruct((p.H, p.BS, p.N), BF16)
    return pl.pallas_call(
        kernel,
        in_specs=[HBM, HBM],
        out_specs=[VM, VM],
        out_shape=[out, out],
        scratch_shapes=[
            pltpu.VMEM((4, step, p.BS, p.N), BF16),
            pltpu.VMEM((4, step, p.BS, p.BS), BF16),
            pltpu.SemaphoreType.DMA((2, 4)),
        ],
        compiler_params=params(8),
        cost_estimate=cost(4 * p.H * p.BS * p.BS * p.N, 6 * p.H * p.BS * p.N),
        name="edge_smooth",
    )(far(rhs), far(smoother))


def row_product(p, blk, i, ext, lcol):
    lhs = jnp.concatenate([blk[i, k] for k in range(p.K)], axis=1)
    rhs = jnp.concatenate([ext[lcol[k, i]] for k in range(p.K)], axis=0)
    return mm(lhs, rhs)


def inner_first(p, pos, cols, counts, sizes, rhs, smoother, blocks, next_inverse):
    piece = 8
    pieces = p.R // piece

    def kernel(
        pos_ref, col_ref, cnt_ref, size_ref, b_hbm, sm_hbm, blk_hbm, inv_hbm,
        b, sm, blk, s2, ext2, acc, lcol, hslot, hcol, hn, bounds, trims, ext, lists, sems, list_sems,
    ):
        start, here = pos_ref[0], pos_ref[1]
        small = [
            pltpu.make_async_copy(src.at[pl.ds(c * piece, piece)], dst.at[pl.ds(c * piece, piece)], sems.at[j, c])
            for c in range(pieces)
            for j, (src, dst) in enumerate(((b_hbm, b), (sm_hbm, sm)))
        ]

        def block_copy(c):
            at = pl.ds(c * piece, piece)
            return pltpu.make_async_copy(blk_hbm.at[at], blk.at[at], sems.at[2, c])

        for c in small:
            c.start()
        inner_pieces = range(p.H // piece, pieces - p.H // piece)
        end_pieces = [c for c in range(pieces) if c not in inner_pieces]
        for c in [*inner_pieces, *end_pieces]:
            block_copy(c).start()
        ext[p.R] = jnp.zeros((p.BS, p.N), BF16)
        ext2[p.R] = jnp.zeros((p.BS, p.N), BF16)

        cols = col_ref[...] - start
        ks = lax.broadcasted_iota(I32, (p.K, p.R), 0)
        live = ks < cnt_ref[...]
        inside = jnp.logical_and(cols >= 0, cols < p.R)
        lists[0] = jnp.where(jnp.logical_and(live, inside), cols, p.R)
        outside = jnp.where(jnp.logical_and(live, jnp.logical_not(inside)), 1, 0)
        place = jnp.where(cols < 0, cols + p.H, cols - p.R + p.H)
        count = jnp.zeros((1, p.R), I32)
        slot_rows = [jnp.zeros((1, p.R), I32)] * p.K
        col_rows = [jnp.full((1, p.R), 2 * p.H, I32)] * p.K
        for k in range(p.K):
            out = outside[k:k + 1]
            for j in range(k + 1):
                mine = jnp.logical_and(out > 0, count == j)
                slot_rows[j] = jnp.where(mine, k, slot_rows[j])
                col_rows[j] = jnp.where(mine, place[k:k + 1], col_rows[j])
            count = count + out
        lists[1] = jnp.concatenate(slot_rows, axis=0)
        lists[2] = jnp.concatenate(col_rows, axis=0)
        lists[3] = jnp.broadcast_to(count, (p.K, p.R))
        list_copies = [
            pltpu.make_async_copy(lists.at[j], dst, list_sems.at[j]) for j, dst in enumerate((lcol, hslot, hcol, hn))
        ]
        for c in list_copies:
            c.start()

        def smooth_row(r, c):
            v = relax_fine * mm(sm[r], b[r])
            s2[r] = v
            ext[r] = v.astype(BF16)
            return c

        for c in range(pieces):
            small[2 * c].wait()
            small[2 * c + 1].wait()
            lax.fori_loop(c * piece, (c + 1) * piece, smooth_row, 0, unroll=8)

        def inner_row(i, c):
            res = b[i].astype(F32) - row_product(p, blk, i, ext, lcol)
            v = s2[i] + relax_fine * mm(sm[i], res.astype(BF16))
            s2[i] = v
            ext2[i] = v.astype(BF16)
            return c

        for c in list_copies:
            c.wait()
        for c in inner_pieces:
            block_copy(c).wait()
            lax.fori_loop(c * piece, (c + 1) * piece, inner_row, 0, unroll=4)

        def edge_row(r, c):
            i = jnp.where(r < p.H, r, r + p.R - 2 * p.H)
            acc[r] = b[i].astype(F32) - row_product(p, blk, i, ext, lcol)
            return c

        for j, c in enumerate(end_pieces):
            block_copy(c).wait()
            lax.fori_loop(j * piece, (j + 1) * piece, edge_row, 0, unroll=4)

        bounds[0] = 0

        def agg(a, t):
            end, first, last, before, after, lowest, highest = t
            begin = end
            end = end + size_ref[0, a]
            bounds[a + 1] = jnp.clip(end, 0, p.R)
            leads = jnp.logical_and(begin <= 0, end > 0)
            ends = jnp.logical_and(begin < p.R, end >= p.R)
            first = jnp.where(leads, end, first)
            last = jnp.where(ends, begin, last)
            lowest = jnp.where(leads, a, lowest)
            highest = jnp.where(ends, a, highest)
            before = jnp.where(jnp.logical_and(begin < 0, end > 0), 1, before)
            after = jnp.where(jnp.logical_and(begin < p.R, end > p.R), 1, after)
            return end, first, last, before, after, lowest, highest

        zero = jnp.int32(0)
        _, first, last, before, after, lowest, highest = lax.fori_loop(0, p.A, agg, (-here * p.R,) + (zero,) * 6)
        trims[0] = jnp.clip(first, 0, p.R)
        trims[1] = jnp.clip(last, 0, p.R)
        trims[2] = before
        trims[3] = after
        trims[4] = lowest
        trims[5] = highest

    ints = lambda n: jax.ShapeDtypeStruct((n,), I32)
    return pl.pallas_call(
        kernel,
        in_specs=[SMEM, VM, VM, SMEM] + [HBM] * 3 + [ANY],
        out_specs=[VM] * 6 + [SMEM] * 6,
        out_shape=[
            pltpu.VMEM(rhs.shape, BF16),
            pltpu.VMEM(smoother.shape, BF16),
            pltpu.VMEM(blocks.shape, BF16),
            pltpu.VMEM((p.R, p.BS, p.N), F32),
            pltpu.VMEM((p.R + 1, p.BS, p.N), BF16),
            pltpu.VMEM((2 * p.H, p.BS, p.N), F32),
            *[jax.ShapeDtypeStruct((p.K, p.R), I32)] * 4,
            ints(p.A + 1),
            ints(6),
        ],
        scratch_shapes=[
            pltpu.VMEM((p.R + 1, p.BS, p.N), BF16),
            pltpu.VMEM((4, p.K, p.R), I32),
            pltpu.SemaphoreType.DMA((3, pieces)),
            pltpu.SemaphoreType.DMA((4,)),
        ],
        compiler_params=params(8),
        cost_estimate=cost(2 * p.R * p.K * p.BS * p.BS * p.N, 2 * p.R * p.K * p.BS * p.BS),
        name="inner_first",
    )(pos, cols, counts, sizes, far(rhs), far(smoother), far(blocks), next_inverse)


GROUP = 4
WIDE = 4


def end_row(p, r):
    return jnp.where(r < p.H, r, r + p.R - 2 * p.H)


def halo_product(hslot, hcol, blk, i, slots, halo):
    lhs = jnp.concatenate([blk[i, hslot[j, i]] for j in slots], axis=1)
    rhs = jnp.concatenate([halo[hcol[j, i]] for j in slots], axis=0)
    return mm(lhs, rhs)


def take_rest(p, hslot, hcol, hn, blk, halo, acc):
    def row(r, c):
        i = end_row(p, r)

        @pl.when(hn[0, i] > WIDE)
        def _():
            acc[r] = acc[r] - halo_product(hslot, hcol, blk, i, range(WIDE, p.K), halo)

        return c

    lax.fori_loop(0, 2 * p.H, row, 0)


def fill_halo(p, before, after, halo):
    halo[:p.H] = before[...]
    halo[p.H:2 * p.H] = after[...]
    halo[2 * p.H] = jnp.zeros((p.BS, p.N), BF16)


def edge_second(p, hslot, hcol, hn, before, after, acc, smoother, blocks, s2, ext2):
    def kernel(hs, hc, hn_ref, bef, aft, acc_in, sm, blk, s2_in, ext_in, s2_out, ext_out, acc_ref, lo, hi, halo, res):
        fill_halo(p, bef, aft, halo)
        take_rest(p, hs, hc, hn_ref, blk, halo, acc_ref)

        def residual(r, c):
            i = end_row(p, r)
            res[r] = (acc_ref[r] - halo_product(hs, hc, blk, i, range(WIDE), halo)).astype(BF16)
            return c

        lax.fori_loop(0, 2 * p.H, residual, 0, unroll=8)

        def sweep(out, r0, i0):
            for g in range(0, p.H, GROUP):
                rows = range(g, g + GROUP)
                new = [s2_in[i0 + r] + relax_fine * mm(sm[i0 + r], res[r0 + r]) for r in rows]
                for r, v in zip(rows, new):
                    s2_out[i0 + r] = v
                    out[r] = v.astype(BF16)
                    ext_out[i0 + r] = v.astype(BF16)

        sweep(lo, 0, 0)
        sweep(hi, p.H, p.R - p.H)

    out = jax.ShapeDtypeStruct((p.H, p.BS, p.N), BF16)
    return pl.pallas_call(
        kernel,
        in_specs=[SMEM] * 3 + [VM] * 7,
        out_specs=[VM] * 5,
        out_shape=[
            pltpu.VMEM((p.R, p.BS, p.N), F32),
            pltpu.VMEM((p.R + 1, p.BS, p.N), BF16),
            pltpu.VMEM((2 * p.H, p.BS, p.N), F32),
            out,
            out,
        ],
        input_output_aliases={8: 0, 9: 1, 5: 2},
        scratch_shapes=[
            pltpu.VMEM((2 * p.H + 1, p.BS, p.N), BF16),
            pltpu.VMEM((2 * p.H, p.BS, p.N), BF16),
        ],
        compiler_params=params(8),
        cost_estimate=cost(8 * p.H * p.BS * p.BS * p.N, 4 * p.H * p.K * p.BS * p.BS),
        name="edge_second",
    )(hslot, hcol, hn, near(before), near(after), near(acc), near(smoother), near(blocks), near(s2), near(ext2))


def aggregate_sum(p, resid, first, last):
    return lax.fori_loop(
        first, last, lambda r, t: t + resid[r].astype(F32), jnp.zeros((p.BS, p.N), F32)
    )


class Rows:
    def __init__(self, fixed, out, sems):
        self.fixed, self.out, self.sems = fixed, out, sems

    def copy(self, r):
        return pltpu.make_async_copy(self.fixed.at[r], self.out.at[r], self.sems.at[r])

    def add(self, p, inverse, res, s2, first, last):
        fix = (relax_coarse * mm(inverse, res)).astype(BF16).astype(F32)

        def row(r, c):
            self.fixed[r] = s2[r] + fix
            self.copy(r).start()
            return c

        lax.fori_loop(first, last, row, 0)

    def wait(self, first, last):
        def row(r, c):
            self.copy(r).wait()
            return c

        lax.fori_loop(first, last, row, 0)


def inner_aggregate(p, first, last):
    return jnp.logical_and(first >= p.H, last <= p.R - p.H)


def fix_aggregates(p, bounds, rows, inv, r2, s2, wanted):
    def chosen(a):
        return jnp.logical_and(bounds[a] < bounds[a + 1], wanted(bounds[a], bounds[a + 1]))

    def one(a, c):
        @pl.when(chosen(a))
        def _():
            res = aggregate_sum(p, r2, bounds[a], bounds[a + 1]).astype(BF16)
            rows.add(p, inv[a], res, s2, bounds[a], bounds[a + 1])

        return c

    lax.fori_loop(0, p.A, one, 0)

    def wait():
        def done(a, c):
            pl.when(chosen(a))(lambda: rows.wait(bounds[a], bounds[a + 1]))
            return c

        lax.fori_loop(0, p.A, done, 0)

    return wait


def rows_scratch(p):
    return [pltpu.VMEM((p.R, p.BS, p.N), F32), pltpu.SemaphoreType.DMA((p.R,))]


def inner_residual(p, pos, lcol, bounds, rhs, blocks, ext2, s2, inverses):
    share = p.A // p.G

    def kernel(pos_ref, lcol_ref, bd, ext, b, blk, s2_ref, *rest):
        inv_refs, (r2, acc, inv, out, fixed, row_sems, sems) = rest[:p.G], rest[p.G:]
        copies = []
        for t in range(p.G):
            place = lax.rem(pos_ref[1] - t + p.G, p.G) * share
            copies.append(pltpu.make_async_copy(inv_refs[t], inv.at[pl.ds(place, share)], sems.at[t]))
        for c in copies:
            c.start()

        def inner_row(i, c):
            r2[i] = (b[i].astype(F32) - row_product(p, blk, i, ext, lcol_ref)).astype(BF16)
            return c

        lax.fori_loop(p.H, p.R - p.H, inner_row, 0, unroll=4)
        for c in copies:
            c.wait()
        rows = Rows(fixed, out, row_sems)
        wait = fix_aggregates(p, bd, rows, inv, r2, s2_ref, lambda first, last: inner_aggregate(p, first, last))

        def edge_row(r, c):
            i = end_row(p, r)
            acc[r] = b[i].astype(F32) - row_product(p, blk, i, ext, lcol_ref)
            return c

        lax.fori_loop(0, 2 * p.H, edge_row, 0, unroll=4)
        wait()

    return pl.pallas_call(
        kernel,
        in_specs=[SMEM] * 3 + [VM] * 4 + [ANY] * p.G,
        out_specs=[VM] * 3 + [HBM],
        out_shape=[
            pltpu.VMEM((p.R, p.BS, p.N), BF16),
            pltpu.VMEM((2 * p.H, p.BS, p.N), F32),
            pltpu.VMEM((p.A, p.BS, p.BS), BF16),
            jax.ShapeDtypeStruct((p.R, p.BS, p.N), F32),
        ],
        scratch_shapes=rows_scratch(p) + [pltpu.SemaphoreType.DMA((p.G,))],
        compiler_params=params(8),
        cost_estimate=cost(2 * p.R * p.K * p.BS * p.BS * p.N, 2 * p.R * p.K * p.BS * p.BS),
        name="inner_residual",
    )(pos, lcol, bounds, near(ext2), near(rhs), near(blocks), near(s2), *inverses)


def edge_final(p, hslot, hcol, hn, trims, before, after, acc, blocks, r2):
    def kernel(hs, hc, hn_ref, trim, bef, aft, acc_in, blk, r2_in, r2_out, acc_ref, part_first, part_last, halo):
        fill_halo(p, bef, aft, halo)
        take_rest(p, hs, hc, hn_ref, blk, halo, acc_ref)

        def row(r, c):
            i = end_row(p, r)
            r2_out[i] = (acc_ref[r] - halo_product(hs, hc, blk, i, range(WIDE), halo)).astype(BF16)
            return c

        lax.fori_loop(0, 2 * p.H, row, 0, unroll=8)
        part_first[...] = aggregate_sum(p, r2_out, 0, trim[0]).astype(BF16)
        part_last[...] = aggregate_sum(p, r2_out, trim[1], p.R).astype(BF16)

    one = jax.ShapeDtypeStruct((p.BS, p.N), BF16)
    return pl.pallas_call(
        kernel,
        in_specs=[SMEM] * 4 + [VM] * 5,
        out_specs=[VM] * 4,
        out_shape=[
            pltpu.VMEM((p.R, p.BS, p.N), BF16),
            pltpu.VMEM((2 * p.H, p.BS, p.N), F32),
            one,
            one,
        ],
        input_output_aliases={8: 0, 6: 1},
        scratch_shapes=[pltpu.VMEM((2 * p.H + 1, p.BS, p.N), BF16)],
        compiler_params=params(8),
        cost_estimate=cost(4 * p.H * p.BS * p.BS * p.N, 4 * p.H * p.K * p.BS * p.BS),
        name="edge_final",
    )(hslot, hcol, hn, trims, near(before), near(after), near(acc), near(blocks), near(r2))


def coarse_own(p, bounds, trims, r2, s2, inv, out):
    def kernel(bd, trim, r2_ref, s2_ref, inv_ref, out_in, out_ref, fixed, row_sems):
        rows = Rows(fixed, out_ref, row_sems)

        def wanted(first, last):
            split = jnp.logical_or(
                jnp.logical_and(first == 0, trim[2] > 0), jnp.logical_and(last == p.R, trim[3] > 0)
            )
            return jnp.logical_not(jnp.logical_or(split, inner_aggregate(p, first, last)))

        fix_aggregates(p, bd, rows, inv_ref, r2_ref, s2_ref, wanted)()

    return pl.pallas_call(
        kernel,
        in_specs=[SMEM] * 2 + [VM] * 3 + [HBM],
        out_specs=HBM,
        out_shape=jax.ShapeDtypeStruct((p.R, p.BS, p.N), F32),
        input_output_aliases={5: 0},
        scratch_shapes=rows_scratch(p),
        compiler_params=params(8),
        cost_estimate=cost(p.A * p.BS * p.BS * p.N, 5 * p.R * p.BS * p.N),
        name="coarse_own",
    )(bounds, trims, near(r2), near(s2), near(inv), out)


def coarse_split(p, bounds, trims, part_first, part_last, from_before, from_after, s2, inv, out):
    def kernel(bd, trim, first_ref, last_ref, bef, aft, s2_ref, inv_ref, out_in, out_ref, fixed, row_sems):
        rows = Rows(fixed, out_ref, row_sems)

        @pl.when(trim[2] > 0)
        def _():
            res = (bef[...].astype(F32) + first_ref[...].astype(F32)).astype(BF16)
            rows.add(p, inv_ref[trim[4]], res, s2_ref, 0, trim[0])

        @pl.when(trim[3] > 0)
        def _():
            res = (last_ref[...].astype(F32) + aft[...].astype(F32)).astype(BF16)
            rows.add(p, inv_ref[trim[5]], res, s2_ref, trim[1], p.R)

        pl.when(trim[2] > 0)(lambda: rows.wait(0, trim[0]))
        pl.when(trim[3] > 0)(lambda: rows.wait(trim[1], p.R))

    return pl.pallas_call(
        kernel,
        in_specs=[SMEM] * 2 + [VM] * 6 + [HBM],
        out_specs=HBM,
        out_shape=jax.ShapeDtypeStruct((p.R, p.BS, p.N), F32),
        input_output_aliases={8: 0},
        scratch_shapes=rows_scratch(p),
        compiler_params=params(8),
        cost_estimate=cost(4 * p.BS * p.BS * p.N, p.R * p.BS * p.N),
        name="coarse_split",
    )(
        bounds, trims, near(part_first), near(part_last), near(from_before), near(from_after), near(s2), near(inv), out
    )


def shift(value, axis, up):
    size = lax.axis_size(axis)
    pairs = [(i, i + 1) for i in range(size - 1)]
    return lax.ppermute(value, axis, pairs if up else [(j, i) for i, j in pairs])


def body(load_rhs, blocks, columns, counts, smoother, agg_sizes, coarse_inv):
    rows, bs, n = load_rhs.shape
    group = lax.axis_size("agg")
    p = Sizes(rows, blocks.shape[1], bs, n, agg_sizes.shape[1], group)
    here = lax.axis_index("agg")
    pos = jnp.stack([lax.axis_index(AXES) * rows, here]).astype(I32)

    lo1, hi1 = edge_smooth(p, load_rhs, smoother)
    before1, after1 = shift(hi1, AXES, True), shift(lo1, AXES, False)
    turn = lambda v, t: lax.ppermute(v, "agg", [(i, (i + t) % group) for i in range(group)])
    inverses = [coarse_inv, turn(coarse_inv, 1)]
    rhs, smoother, blocks, s2, ext2, acc1, lcol, hslot, hcol, hn, bounds, trims = inner_first(
        p, pos, columns.T, counts[None, :], agg_sizes, load_rhs, smoother, blocks, inverses[1]
    )
    late, hn = lax.optimization_barrier((coarse_inv, hn))
    inverses += [turn(late, t) for t in range(2, group)]

    s2, ext2, _, lo2, hi2 = edge_second(p, hslot, hcol, hn, before1, after1, acc1, smoother, blocks, s2, ext2)
    before2, after2 = shift(hi2, AXES, True), shift(lo2, AXES, False)
    r2, acc2, inv, out = inner_residual(p, pos, lcol, bounds, rhs, blocks, ext2, s2, inverses)
    r2, _, part_first, part_last = edge_final(p, hslot, hcol, hn, trims, before2, after2, acc2, blocks, r2)
    from_before, from_after = shift(part_last, "agg", True), shift(part_first, "agg", False)
    out = coarse_own(p, bounds, trims, r2, s2, inv, out)
    return coarse_split(p, bounds, trims, part_first, part_last, from_before, from_after, s2, inv, out)


def solution(mesh):
    placed = (
        P(AXES, None, None),
        P(AXES, None, None, None),
        P(AXES, None),
        P(AXES),
        P(AXES, None, None),
        P("rows", None),
        P(AXES, None, None),
    )
    return jax.shard_map(
        body, mesh=mesh, in_specs=placed, out_specs=P(AXES, None, None), check_vma=False
    )
```

```python
import jax
import jax.numpy as jnp
from jax import lax
from jax.experimental import pallas as pl
from jax.experimental.pallas import tpu as pltpu
from jax.sharding import PartitionSpec as P

HALO = 16

relax_fine = 0.8
relax_coarse = 1.0

AXES = ("rows", "agg")
F32 = jnp.float32
BF16 = jnp.bfloat16
I32 = jnp.int32
MIB = 1024 * 1024
WEIGHT = 32

SMEM = pl.BlockSpec(memory_space=pltpu.SMEM)
VM = pl.BlockSpec(memory_space=pltpu.VMEM)
ANY = pl.BlockSpec(memory_space=pl.ANY)
HBM = pl.BlockSpec(memory_space=pltpu.HBM)


def mm(a, b):
    return jnp.dot(a, b, preferred_element_type=F32)


def cost(flops, nbytes):
    return pl.CostEstimate(flops=WEIGHT * flops, bytes_accessed=nbytes, transcendentals=0)


def params(mib):
    return pltpu.CompilerParams(vmem_limit_bytes=mib * MIB)


def near(x):
    return pltpu.with_memory_space_constraint(x, pltpu.VMEM)


def far(x):
    return pltpu.with_memory_space_constraint(x, pltpu.HBM)


class Sizes:
    def __init__(self, rows, slots, bs, n, aggs, group):
        self.R, self.K, self.BS, self.N, self.A, self.G = rows, slots, bs, n, aggs, group
        self.H = HALO


def edge_smooth(p, rhs, smoother):
    step = 8
    starts = [0, step, p.R - p.H, p.R - p.H + step]

    def kernel(b_hbm, s_hbm, lo_ref, hi_ref, b, s, sems):
        copies = []
        for c, at in enumerate(starts):
            copies.append(pltpu.make_async_copy(b_hbm.at[pl.ds(at, step)], b.at[c], sems.at[0, c]))
            copies.append(pltpu.make_async_copy(s_hbm.at[pl.ds(at, step)], s.at[c], sems.at[1, c]))
        for c in copies:
            c.start()
        for c in range(len(starts)):
            copies[2 * c].wait()
            copies[2 * c + 1].wait()
            out = lo_ref if c < 2 else hi_ref
            for r in range(step):
                out[(c % 2) * step + r] = (relax_fine * mm(s[c, r], b[c, r])).astype(BF16)

    out = jax.ShapeDtypeStruct((p.H, p.BS, p.N), BF16)
    return pl.pallas_call(
        kernel,
        in_specs=[HBM, HBM],
        out_specs=[VM, VM],
        out_shape=[out, out],
        scratch_shapes=[
            pltpu.VMEM((4, step, p.BS, p.N), BF16),
            pltpu.VMEM((4, step, p.BS, p.BS), BF16),
            pltpu.SemaphoreType.DMA((2, 4)),
        ],
        compiler_params=params(8),
        cost_estimate=cost(4 * p.H * p.BS * p.BS * p.N, 6 * p.H * p.BS * p.N),
        name="edge_smooth",
    )(far(rhs), far(smoother))


def end_row(p, r):
    return jnp.where(r < p.H, r, r + p.R - 2 * p.H)


def row_product(p, blk, at, i, ext, lcol):
    lhs = jnp.concatenate([blk[at, k] for k in range(p.K)], axis=1)
    rhs = jnp.concatenate([ext[lcol[k, i]] for k in range(p.K)], axis=0)
    return mm(lhs, rhs)


def first_sweep(p, pos, cols, counts, sizes, rhs, smoother, blocks, distant):
    piece = 8
    pieces = p.R // piece
    end_pieces = 2 * p.H // piece

    def kernel(
        pos_ref, col_ref, cnt_ref, size_ref, b_hbm, sm_hbm, blk_hbm, _,
        b, sm, blk, s2, ext, acc, lcol, hslot, hcol, hn, bounds, trims, lists, sems, list_sems,
    ):
        start, here = pos_ref[0], pos_ref[1]
        small = [
            pltpu.make_async_copy(src.at[pl.ds(c * piece, piece)], dst.at[pl.ds(c * piece, piece)], sems.at[j, c])
            for c in range(pieces)
            for j, (src, dst) in enumerate(((b_hbm, b), (sm_hbm, sm)))
        ]

        def block_copy(c):
            src = pl.ds(c * piece if c < end_pieces // 2 else p.R - 2 * p.H + c * piece, piece)
            return pltpu.make_async_copy(blk_hbm.at[src], blk.at[pl.ds(c * piece, piece)], sems.at[2, c])

        for c in small:
            c.start()
        for c in range(end_pieces):
            block_copy(c).start()
        ext[p.R] = jnp.zeros((p.BS, p.N), BF16)

        cols = col_ref[...] - start
        ks = lax.broadcasted_iota(I32, (p.K, p.R), 0)
        live = ks < cnt_ref[...]
        inside = jnp.logical_and(cols >= 0, cols < p.R)
        lists[0] = jnp.where(jnp.logical_and(live, inside), cols, p.R)
        outside = jnp.where(jnp.logical_and(live, jnp.logical_not(inside)), 1, 0)
        place = jnp.where(cols < 0, cols + p.H, cols - p.R + p.H)
        count = jnp.zeros((1, p.R), I32)
        slot_rows = [jnp.zeros((1, p.R), I32)] * p.K
        col_rows = [jnp.full((1, p.R), 2 * p.H, I32)] * p.K
        for k in range(p.K):
            out = outside[k:k + 1]
            for j in range(k + 1):
                mine = jnp.logical_and(out > 0, count == j)
                slot_rows[j] = jnp.where(mine, k, slot_rows[j])
                col_rows[j] = jnp.where(mine, place[k:k + 1], col_rows[j])
            count = count + out
        lists[1] = jnp.concatenate(slot_rows, axis=0)
        lists[2] = jnp.concatenate(col_rows, axis=0)
        lists[3] = jnp.broadcast_to(count, (p.K, p.R))
        list_copies = [
            pltpu.make_async_copy(lists.at[j], dst, list_sems.at[j]) for j, dst in enumerate((lcol, hslot, hcol, hn))
        ]
        for c in list_copies:
            c.start()

        def smooth_row(r, c):
            v = relax_fine * mm(sm[r], b[r])
            s2[r] = v
            ext[r] = v.astype(BF16)
            return c

        for c in range(pieces):
            small[2 * c].wait()
            small[2 * c + 1].wait()
            lax.fori_loop(c * piece, (c + 1) * piece, smooth_row, 0, unroll=8)

        for c in list_copies:
            c.wait()

        def edge_row(r, c):
            i = end_row(p, r)
            acc[r] = b[i].astype(F32) - row_product(p, blk, r, i, ext, lcol)
            return c

        for c in range(end_pieces):
            block_copy(c).wait()
            lax.fori_loop(c * piece, (c + 1) * piece, edge_row, 0, unroll=4)

        bounds[0] = 0

        def agg(a, t):
            end, first, last, before, after, lowest, highest = t
            begin = end
            end = end + size_ref[0, a]
            bounds[a + 1] = jnp.clip(end, 0, p.R)
            leads = jnp.logical_and(begin <= 0, end > 0)
            ends = jnp.logical_and(begin < p.R, end >= p.R)
            first = jnp.where(leads, end, first)
            last = jnp.where(ends, begin, last)
            lowest = jnp.where(leads, a, lowest)
            highest = jnp.where(ends, a, highest)
            before = jnp.where(jnp.logical_and(begin < 0, end > 0), 1, before)
            after = jnp.where(jnp.logical_and(begin < p.R, end > p.R), 1, after)
            return end, first, last, before, after, lowest, highest

        zero = jnp.int32(0)
        _, first, last, before, after, lowest, highest = lax.fori_loop(0, p.A, agg, (-here * p.R,) + (zero,) * 6)
        trims[0] = jnp.clip(first, 0, p.R)
        trims[1] = jnp.clip(last, 0, p.R)
        trims[2] = before
        trims[3] = after
        trims[4] = lowest
        trims[5] = highest

    ints = lambda n: jax.ShapeDtypeStruct((n,), I32)
    return pl.pallas_call(
        kernel,
        in_specs=[SMEM, VM, VM, SMEM] + [HBM] * 4,
        out_specs=[VM] * 6 + [SMEM] * 6,
        out_shape=[
            pltpu.VMEM(rhs.shape, BF16),
            pltpu.VMEM(smoother.shape, BF16),
            pltpu.VMEM((2 * p.H,) + blocks.shape[1:], BF16),
            pltpu.VMEM((p.R, p.BS, p.N), F32),
            pltpu.VMEM((p.R + 1, p.BS, p.N), BF16),
            pltpu.VMEM((2 * p.H, p.BS, p.N), F32),
            *[jax.ShapeDtypeStruct((p.K, p.R), I32)] * 4,
            ints(p.A + 1),
            ints(6),
        ],
        scratch_shapes=[
            pltpu.VMEM((4, p.K, p.R), I32),
            pltpu.SemaphoreType.DMA((3, pieces)),
            pltpu.SemaphoreType.DMA((4,)),
        ],
        compiler_params=params(8),
        cost_estimate=cost(2 * p.R * p.K * p.BS * p.BS * p.N, 2 * p.R * p.K * p.BS * p.BS),
        name="first_sweep",
    )(pos, cols, counts, sizes, far(rhs), far(smoother), far(blocks), far(distant))


GROUP = 4
WIDE = 4


def halo_product(hslot, hcol, blk, r, i, slots, halo):
    lhs = jnp.concatenate([blk[r, hslot[j, i]] for j in slots], axis=1)
    rhs = jnp.concatenate([halo[hcol[j, i]] for j in slots], axis=0)
    return mm(lhs, rhs)


def take_rest(p, hslot, hcol, hn, blk, halo, acc):
    def row(r, c):
        i = end_row(p, r)

        @pl.when(hn[0, i] > WIDE)
        def _():
            acc[r] = acc[r] - halo_product(hslot, hcol, blk, r, i, range(WIDE, p.K), halo)

        return c

    lax.fori_loop(0, 2 * p.H, row, 0)


def fill_halo(p, before, after, halo):
    halo[:p.H] = before[...]
    halo[p.H:2 * p.H] = after[...]
    halo[2 * p.H] = jnp.zeros((p.BS, p.N), BF16)


def edge_second(p, hslot, hcol, hn, before, after, acc, smoother, blocks, s2):
    def kernel(hs, hc, hn_ref, bef, aft, acc_in, sm, blk, s2_in, s2_out, ext_out, acc_ref, lo, hi, halo, res):
        fill_halo(p, bef, aft, halo)
        take_rest(p, hs, hc, hn_ref, blk, halo, acc_ref)

        def residual(r, c):
            i = end_row(p, r)
            res[r] = (acc_ref[r] - halo_product(hs, hc, blk, r, i, range(WIDE), halo)).astype(BF16)
            return c

        lax.fori_loop(0, 2 * p.H, residual, 0, unroll=8)

        def sweep(out, r0, i0):
            for g in range(0, p.H, GROUP):
                rows = range(g, g + GROUP)
                new = [s2_in[i0 + r] + relax_fine * mm(sm[i0 + r], res[r0 + r]) for r in rows]
                for r, v in zip(rows, new):
                    s2_out[i0 + r] = v
                    out[r] = v.astype(BF16)
                    ext_out[i0 + r] = v.astype(BF16)

        sweep(lo, 0, 0)
        sweep(hi, p.H, p.R - p.H)
        ext_out[p.R] = jnp.zeros((p.BS, p.N), BF16)

    out = jax.ShapeDtypeStruct((p.H, p.BS, p.N), BF16)
    return pl.pallas_call(
        kernel,
        in_specs=[SMEM] * 3 + [VM] * 6,
        out_specs=[VM] * 5,
        out_shape=[
            pltpu.VMEM((p.R, p.BS, p.N), F32),
            pltpu.VMEM((p.R + 1, p.BS, p.N), BF16),
            pltpu.VMEM((2 * p.H, p.BS, p.N), F32),
            out,
            out,
        ],
        input_output_aliases={8: 0, 5: 2},
        scratch_shapes=[
            pltpu.VMEM((2 * p.H + 1, p.BS, p.N), BF16),
            pltpu.VMEM((2 * p.H, p.BS, p.N), BF16),
        ],
        compiler_params=params(8),
        cost_estimate=cost(8 * p.H * p.BS * p.BS * p.N, 4 * p.H * p.K * p.BS * p.BS),
        name="edge_second",
    )(hslot, hcol, hn, near(before), near(after), near(acc), near(smoother), near(blocks), near(s2))


def aggregate_sum(p, resid, first, last):
    return lax.fori_loop(
        first, last, lambda r, t: t + resid[r].astype(F32), jnp.zeros((p.BS, p.N), F32)
    )


def add_fix(inverse, res, s2, first, last):
    fix = (relax_coarse * mm(inverse, res)).astype(BF16).astype(F32)

    def row(r, c):
        s2[r] = s2[r] + fix
        return c

    lax.fori_loop(first, last, row, 0)


def inner_aggregate(p, first, last):
    return jnp.logical_and(first >= p.H, last <= p.R - p.H)


def inner_rows(p, pos, lcol, bounds, rhs, smoother, end_blocks, blocks, ext1, ext2, s2, inverses):
    piece = 4
    inner = p.R - 2 * p.H
    share = p.A // p.G

    def kernel(pos_ref, lcol_ref, bd, b, sm, end_blk, ext1_ref, ext_in, s2_ref, blk_hbm, *rest):
        inv_refs, (r2, acc, inv, ext, s2_out, out, blk, row_sems, sems, blk_sems) = rest[:4], rest[4:]

        def block_copy(c):
            src = blk_hbm.at[pl.ds(p.H + c * piece, piece)]
            return pltpu.make_async_copy(src, blk.at[pl.ds(c * piece, piece)], blk_sems.at[c])

        for c in range(inner // piece):
            block_copy(c).start()

        own, before, after, distant = inv_refs

        def place(src, t):
            at = pl.ds(lax.rem(pos_ref[1] - t + p.G, p.G) * share, share)
            return pltpu.make_async_copy(src, inv.at[at], sems.at[t])

        def place_all(act):
            act(place(own, 0))

            @pl.when(pos_ref[2] == 0)
            def _():
                act(place(before, 1))
                act(place(after, p.G - 1))

            @pl.when(pos_ref[2] > 0)
            def _():
                for t in range(1, p.G):
                    act(place(distant.at[t - 1], t))

        place_all(lambda c: c.start())

        for c in range(inner // piece):
            block_copy(c).wait()
            rows = range(c * piece, (c + 1) * piece)
            res = [
                (b[p.H + r].astype(F32) - row_product(p, blk, r, p.H + r, ext1_ref, lcol_ref)).astype(BF16) for r in rows
            ]
            new = [s2_ref[p.H + r] + relax_fine * mm(sm[p.H + r], v) for r, v in zip(rows, res)]
            for r, v in zip(rows, new):
                s2_out[p.H + r] = v
                ext[p.H + r] = v.astype(BF16)

        def inner_row(r, c):
            i = p.H + r
            r2[i] = (b[i].astype(F32) - row_product(p, blk, r, i, ext, lcol_ref)).astype(BF16)
            return c

        lax.fori_loop(0, inner, inner_row, 0, unroll=4)
        place_all(lambda c: c.wait())

        def copy(r):
            return pltpu.make_async_copy(s2_out.at[r], out.at[r], row_sems.at[r])

        def send(r, c):
            copy(r).start()
            return c

        def wait(r, c):
            copy(r).wait()
            return c

        def aggregates(act):
            def one(a, c):
                first, last = bd[a], bd[a + 1]
                pl.when(jnp.logical_and(first < last, inner_aggregate(p, first, last)))(lambda: act(a, first, last))
                return c

            lax.fori_loop(0, p.A, one, 0)

        def fix(a, first, last):
            res = aggregate_sum(p, r2, first, last).astype(BF16)
            add_fix(inv[a], res, s2_out, first, last)
            lax.fori_loop(first, last, send, 0)

        aggregates(fix)

        def edge_row(r, c):
            i = end_row(p, r)
            acc[r] = b[i].astype(F32) - row_product(p, end_blk, r, i, ext, lcol_ref)
            return c

        lax.fori_loop(0, 2 * p.H, edge_row, 0, unroll=4)

        def settle(a, first, last):
            lax.fori_loop(first, last, wait, 0)

        aggregates(settle)

    return pl.pallas_call(
        kernel,
        in_specs=[SMEM] * 3 + [VM] * 6 + [HBM] + [ANY] * 3 + [HBM],
        out_specs=[VM] * 5 + [HBM],
        out_shape=[
            pltpu.VMEM((p.R, p.BS, p.N), BF16),
            pltpu.VMEM((2 * p.H, p.BS, p.N), F32),
            pltpu.VMEM((p.A, p.BS, p.BS), BF16),
            pltpu.VMEM((p.R + 1, p.BS, p.N), BF16),
            pltpu.VMEM((p.R, p.BS, p.N), F32),
            jax.ShapeDtypeStruct((p.R, p.BS, p.N), F32),
        ],
        input_output_aliases={7: 3, 8: 4},
        scratch_shapes=[
            pltpu.VMEM((inner,) + blocks.shape[1:], BF16),
            pltpu.SemaphoreType.DMA((p.R,)),
            pltpu.SemaphoreType.DMA((p.G,)),
            pltpu.SemaphoreType.DMA((inner // piece,)),
        ],
        compiler_params=params(16),
        cost_estimate=cost(2 * p.R * p.K * p.BS * p.BS * p.N, 2 * p.R * p.K * p.BS * p.BS),
        name="inner_rows",
    )(
        pos, lcol, bounds, near(rhs), near(smoother), near(end_blocks), near(ext1), near(ext2), near(s2), far(blocks),
        *inverses[:3], far(inverses[3]),
    )


def edge_final(p, hslot, hcol, hn, trims, before, after, acc, blocks, r2):
    def kernel(hs, hc, hn_ref, trim, bef, aft, acc_in, blk, r2_in, r2_out, acc_ref, part_first, part_last, halo):
        fill_halo(p, bef, aft, halo)
        take_rest(p, hs, hc, hn_ref, blk, halo, acc_ref)

        def row(r, c):
            i = end_row(p, r)
            r2_out[i] = (acc_ref[r] - halo_product(hs, hc, blk, r, i, range(WIDE), halo)).astype(BF16)
            return c

        lax.fori_loop(0, 2 * p.H, row, 0, unroll=8)
        part_first[...] = aggregate_sum(p, r2_out, 0, trim[0]).astype(BF16)
        part_last[...] = aggregate_sum(p, r2_out, trim[1], p.R).astype(BF16)

    one = jax.ShapeDtypeStruct((p.BS, p.N), BF16)
    return pl.pallas_call(
        kernel,
        in_specs=[SMEM] * 4 + [VM] * 5,
        out_specs=[VM] * 4,
        out_shape=[
            pltpu.VMEM((p.R, p.BS, p.N), BF16),
            pltpu.VMEM((2 * p.H, p.BS, p.N), F32),
            one,
            one,
        ],
        input_output_aliases={8: 0, 6: 1},
        scratch_shapes=[pltpu.VMEM((2 * p.H + 1, p.BS, p.N), BF16)],
        compiler_params=params(8),
        cost_estimate=cost(4 * p.H * p.BS * p.BS * p.N, 4 * p.H * p.K * p.BS * p.BS),
        name="edge_final",
    )(hslot, hcol, hn, trims, near(before), near(after), near(acc), near(blocks), near(r2))


def coarse_own(p, bounds, trims, r2, s2, inv):
    def kernel(bd, trim, r2_ref, s2_in, inv_ref, s2_ref):
        def one(a, c):
            first, last = bd[a], bd[a + 1]
            split = jnp.logical_or(
                jnp.logical_and(first == 0, trim[2] > 0), jnp.logical_and(last == p.R, trim[3] > 0)
            )
            done = jnp.logical_or(split, inner_aggregate(p, first, last))

            @pl.when(jnp.logical_and(first < last, jnp.logical_not(done)))
            def _():
                res = aggregate_sum(p, r2_ref, first, last).astype(BF16)
                add_fix(inv_ref[a], res, s2_ref, first, last)

            return c

        lax.fori_loop(0, p.A, one, 0)

    return pl.pallas_call(
        kernel,
        in_specs=[SMEM] * 2 + [VM] * 3,
        out_specs=VM,
        out_shape=pltpu.VMEM((p.R, p.BS, p.N), F32),
        input_output_aliases={3: 0},
        compiler_params=params(8),
        cost_estimate=cost(p.A * p.BS * p.BS * p.N, 5 * p.R * p.BS * p.N),
        name="coarse_own",
    )(bounds, trims, near(r2), near(s2), near(inv))


def coarse_split(p, bounds, trims, part_first, part_last, from_before, from_after, s2, inv, out):
    def kernel(bd, trim, first_ref, last_ref, bef, aft, s2_in, inv_ref, out_in, s2_ref, out_ref, row_sems):
        @pl.when(trim[2] > 0)
        def _():
            res = (bef[...].astype(F32) + first_ref[...].astype(F32)).astype(BF16)
            add_fix(inv_ref[trim[4]], res, s2_ref, 0, trim[0])

        @pl.when(trim[3] > 0)
        def _():
            res = (last_ref[...].astype(F32) + aft[...].astype(F32)).astype(BF16)
            add_fix(inv_ref[trim[5]], res, s2_ref, trim[1], p.R)

        def inner(a, t):
            begin, end = t
            first, last = bd[a], bd[a + 1]
            sent = jnp.logical_and(first < last, inner_aggregate(p, first, last))
            return jnp.where(sent, jnp.minimum(begin, first), begin), jnp.where(sent, last, end)

        begin, end = lax.fori_loop(0, p.A, inner, (jnp.int32(p.R), jnp.int32(p.R)))

        def copy(r):
            return pltpu.make_async_copy(s2_ref.at[r], out_ref.at[r], row_sems.at[r])

        def send(r, c):
            copy(r).start()
            return c

        def wait(r, c):
            copy(r).wait()
            return c

        for step in (send, wait):
            lax.fori_loop(0, begin, step, 0)
            lax.fori_loop(end, p.R, step, 0)

    return pl.pallas_call(
        kernel,
        in_specs=[SMEM] * 2 + [VM] * 6 + [HBM],
        out_specs=[VM, HBM],
        out_shape=[
            pltpu.VMEM((p.R, p.BS, p.N), F32),
            jax.ShapeDtypeStruct((p.R, p.BS, p.N), F32),
        ],
        input_output_aliases={6: 0, 8: 1},
        scratch_shapes=[pltpu.SemaphoreType.DMA((p.R,))],
        compiler_params=params(8),
        cost_estimate=cost(4 * p.BS * p.BS * p.N, p.R * p.BS * p.N),
        name="coarse_split",
    )(
        bounds, trims, near(part_first), near(part_last), near(from_before), near(from_after), near(s2), near(inv), out
    )[1]


def shift(value, axis, up):
    size = lax.axis_size(axis)
    pairs = [(i, i + 1) for i in range(size - 1)]
    return lax.ppermute(value, axis, pairs if up else [(j, i) for i, j in pairs])


def body(load_rhs, blocks, columns, counts, smoother, agg_sizes, coarse_inv):
    rows, bs, n = load_rhs.shape
    group = lax.axis_size("agg")
    p = Sizes(rows, blocks.shape[1], bs, n, agg_sizes.shape[1], group)
    here = lax.axis_index("agg")

    lo1, hi1 = edge_smooth(p, load_rhs, smoother)
    before1, after1 = shift(hi1, AXES, True), shift(lo1, AXES, False)

    sizes, own_inv, lo1 = lax.optimization_barrier((agg_sizes, coarse_inv, lo1))
    ids = jnp.arange(p.A, dtype=I32)
    ends = jnp.sum(jnp.where(ids[None, :] <= ids[:, None], sizes, 0), axis=1)
    owner = ids // (p.A // group)
    reach = jnp.maximum((ends - 1) // rows - owner, owner - (ends - sizes[0]) // rows)
    apart = jnp.max(reach) > 1

    def every(own):
        turn = lambda t: lax.ppermute(own, "agg", [(i, (i + t) % group) for i in range(group)])
        return jnp.stack([turn(t) for t in range(1, group)])

    def none(own):
        return jnp.zeros((group - 1,) + own.shape, own.dtype)

    distant = lax.cond(apart, every, none, own_inv)
    pos = jnp.stack([lax.axis_index(AXES) * rows, here, apart.astype(I32)]).astype(I32)
    rhs, smoother, end_blocks, s2, ext1, acc1, lcol, hslot, hcol, hn, bounds, trims = first_sweep(
        p, pos, columns.T, counts[None, :], agg_sizes, load_rhs, smoother, blocks, distant
    )
    late, hn = lax.optimization_barrier((coarse_inv, hn))
    inverses = coarse_inv, shift(late, "agg", True), shift(late, "agg", False), distant

    s2, ext2, _, lo2, hi2 = edge_second(p, hslot, hcol, hn, before1, after1, acc1, smoother, end_blocks, s2)
    before2, after2 = shift(hi2, AXES, True), shift(lo2, AXES, False)
    r2, acc2, inv, _, s2, out = inner_rows(
        p, pos, lcol, bounds, rhs, smoother, end_blocks, blocks, ext1, ext2, s2, inverses
    )
    r2, _, part_first, part_last = edge_final(p, hslot, hcol, hn, trims, before2, after2, acc2, end_blocks, r2)
    from_before, from_after = shift(part_last, "agg", True), shift(part_first, "agg", False)
    s2 = coarse_own(p, bounds, trims, r2, s2, inv)
    return coarse_split(p, bounds, trims, part_first, part_last, from_before, from_after, s2, inv, out)


def solution(mesh):
    placed = (
        P(AXES, None, None),
        P(AXES, None, None, None),
        P(AXES, None),
        P(AXES),
        P(AXES, None, None),
        P("rows", None),
        P(AXES, None, None),
    )
    return jax.shard_map(
        body, mesh=mesh, in_specs=placed, out_specs=P(AXES, None, None), check_vma=False
    )
```

```python
import jax
import jax.numpy as jnp
from jax import lax
from jax.experimental import pallas as pl
from jax.experimental.pallas import tpu as pltpu
from jax.sharding import PartitionSpec as P

HALO = 16

relax_fine = 0.8
relax_coarse = 1.0

AXES = ("rows", "agg")
F32 = jnp.float32
BF16 = jnp.bfloat16
I32 = jnp.int32
MIB = 1024 * 1024
WEIGHT = 32

SMEM = pl.BlockSpec(memory_space=pltpu.SMEM)
VM = pl.BlockSpec(memory_space=pltpu.VMEM)
ANY = pl.BlockSpec(memory_space=pl.ANY)
HBM = pl.BlockSpec(memory_space=pltpu.HBM)


def mm(a, b):
    return jnp.dot(a, b, preferred_element_type=F32)


def cost(flops, nbytes):
    return pl.CostEstimate(flops=WEIGHT * flops, bytes_accessed=nbytes, transcendentals=0)


def params(mib):
    return pltpu.CompilerParams(vmem_limit_bytes=mib * MIB)


def near(x):
    return pltpu.with_memory_space_constraint(x, pltpu.VMEM)


def far(x):
    return pltpu.with_memory_space_constraint(x, pltpu.HBM)


class Sizes:
    def __init__(self, rows, slots, bs, n, aggs, group):
        self.R, self.K, self.BS, self.N, self.A, self.G = rows, slots, bs, n, aggs, group
        self.H = HALO


def edge_smooth(p, pos, sizes, rhs, smoother):
    step = p.H // 2
    share = p.A // p.G

    def kernel(pos_ref, size_ref, b_hbm, s_hbm, apart, *rest):
        outs, (b, s, sems) = rest[:4], rest[4:]
        odd = pos_ref[2]
        starts = []
        for first, last in ((0, p.R - step), (step, p.R - 2 * step)):
            starts += [jnp.where(odd > 0, last, first), jnp.where(odd > 0, first, last)]
        copies = []
        for c, at in enumerate(starts):
            copies.append(pltpu.make_async_copy(b_hbm.at[pl.ds(at, step)], b.at[c], sems.at[0, c]))
            copies.append(pltpu.make_async_copy(s_hbm.at[pl.ds(at, step)], s.at[c], sems.at[1, c]))
        for c in copies:
            c.start()

        def reach(a, t):
            begin, most = t
            end = begin + size_ref[0, a]
            owner = a // share
            here = jnp.maximum(lax.div(end - 1, p.R) - owner, owner - lax.div(begin, p.R))
            return end, jnp.maximum(most, here)

        apart[0] = lax.fori_loop(0, p.A, reach, (jnp.int32(0), jnp.int32(0)))[1]
        for c in range(4):
            copies[2 * c].wait()
            copies[2 * c + 1].wait()
            for r in range(step):
                outs[c][r] = (relax_fine * mm(s[c, r], b[c, r])).astype(BF16)

    out = jax.ShapeDtypeStruct((step, p.BS, p.N), BF16)
    return pl.pallas_call(
        kernel,
        in_specs=[SMEM, SMEM, HBM, HBM],
        out_specs=[SMEM] + [VM] * 4,
        out_shape=[jax.ShapeDtypeStruct((1,), I32)] + [out] * 4,
        scratch_shapes=[
            pltpu.VMEM((4, step, p.BS, p.N), BF16),
            pltpu.VMEM((4, step, p.BS, p.BS), BF16),
            pltpu.SemaphoreType.DMA((2, 4)),
        ],
        compiler_params=params(8),
        cost_estimate=cost(4 * p.H * p.BS * p.BS * p.N, 6 * p.H * p.BS * p.N),
        name="edge_smooth",
    )(pos, sizes, far(rhs), far(smoother))


def end_row(p, r):
    return jnp.where(r < p.H, r, r + p.R - 2 * p.H)


def row_product(p, blk, at, i, ext, lcol):
    lhs = jnp.concatenate([blk[at, k] for k in range(p.K)], axis=1)
    rhs = jnp.concatenate([ext[lcol[k, i]] for k in range(p.K)], axis=0)
    return mm(lhs, rhs)


def first_sweep(p, pos, cols, counts, sizes, rhs, smoother, blocks, apart, inverses):
    piece = 8
    share = p.A // p.G
    pieces = p.R // piece
    end_pieces = 2 * p.H // piece

    def kernel(
        pos_ref, col_ref, cnt_ref, size_ref, b_hbm, sm_hbm, blk_hbm, apart_ref, own, by_odd, by_even, distant,
        b, sm, blk, inv, s2, ext, acc, lcol, hslot, hcol, hn, bounds, trims, lists, sems, list_sems, inv_sems,
    ):
        start, here = pos_ref[0], pos_ref[1]
        small = [
            pltpu.make_async_copy(src.at[pl.ds(c * piece, piece)], dst.at[pl.ds(c * piece, piece)], sems.at[j, c])
            for c in range(pieces)
            for j, (src, dst) in enumerate(((b_hbm, b), (sm_hbm, sm)))
        ]

        def block_copy(c):
            src = pl.ds(c * piece if c < end_pieces // 2 else p.R - 2 * p.H + c * piece, piece)
            return pltpu.make_async_copy(blk_hbm.at[src], blk.at[pl.ds(c * piece, piece)], sems.at[2, c])

        for c in small:
            c.start()
        for c in range(end_pieces):
            block_copy(c).start()
        back = jnp.where((pos_ref[1] & 1) > 0, p.G - 1, 1)

        def inverse_copy(src, distance, t):
            at = pl.ds(lax.rem(pos_ref[1] - distance + p.G, p.G) * share, share)
            return pltpu.make_async_copy(src, inv.at[at], inv_sems.at[t])

        def place_all(act):
            act(inverse_copy(own, 0, 0))

            @pl.when(apart_ref[0] <= 1)
            def _():
                act(inverse_copy(by_odd, back, 1))
                act(inverse_copy(by_even, p.G - back, 2))

            @pl.when(apart_ref[0] > 1)
            def _():
                for t in range(1, p.G):
                    act(inverse_copy(distant.at[t - 1], t, t))

        place_all(lambda c: c.start())
        ext[p.R] = jnp.zeros((p.BS, p.N), BF16)

        cols = col_ref[...] - start
        ks = lax.broadcasted_iota(I32, (p.K, p.R), 0)
        live = ks < cnt_ref[...]
        inside = jnp.logical_and(cols >= 0, cols < p.R)
        lists[0] = jnp.where(jnp.logical_and(live, inside), cols, p.R)
        outside = jnp.where(jnp.logical_and(live, jnp.logical_not(inside)), 1, 0)
        place = jnp.where(cols < 0, cols + p.H, cols - p.R + p.H)
        count = jnp.zeros((1, p.R), I32)
        slot_rows = [jnp.zeros((1, p.R), I32)] * p.K
        col_rows = [jnp.full((1, p.R), 2 * p.H, I32)] * p.K
        for k in range(p.K):
            out = outside[k:k + 1]
            for j in range(k + 1):
                mine = jnp.logical_and(out > 0, count == j)
                slot_rows[j] = jnp.where(mine, k, slot_rows[j])
                col_rows[j] = jnp.where(mine, place[k:k + 1], col_rows[j])
            count = count + out
        lists[1] = jnp.concatenate(slot_rows, axis=0)
        lists[2] = jnp.concatenate(col_rows, axis=0)
        lists[3] = jnp.broadcast_to(count, (p.K, p.R))
        list_copies = [
            pltpu.make_async_copy(lists.at[j], dst, list_sems.at[j]) for j, dst in enumerate((lcol, hslot, hcol, hn))
        ]
        for c in list_copies:
            c.start()

        def smooth_row(r, c):
            v = relax_fine * mm(sm[r], b[r])
            s2[r] = v
            ext[r] = v.astype(BF16)
            return c

        for c in range(pieces):
            small[2 * c].wait()
            small[2 * c + 1].wait()
            lax.fori_loop(c * piece, (c + 1) * piece, smooth_row, 0, unroll=8)

        for c in list_copies:
            c.wait()

        def edge_row(r, c):
            i = end_row(p, r)
            acc[r] = b[i].astype(F32) - row_product(p, blk, r, i, ext, lcol)
            return c

        for c in range(end_pieces):
            block_copy(c).wait()
            lax.fori_loop(c * piece, (c + 1) * piece, edge_row, 0, unroll=4)

        place_all(lambda c: c.wait())

        bounds[0] = 0

        def agg(a, t):
            end, first, last, before, after, lowest, highest = t
            begin = end
            end = end + size_ref[0, a]
            bounds[a + 1] = jnp.clip(end, 0, p.R)
            leads = jnp.logical_and(begin <= 0, end > 0)
            ends = jnp.logical_and(begin < p.R, end >= p.R)
            first = jnp.where(leads, end, first)
            last = jnp.where(ends, begin, last)
            lowest = jnp.where(leads, a, lowest)
            highest = jnp.where(ends, a, highest)
            before = jnp.where(jnp.logical_and(begin < 0, end > 0), 1, before)
            after = jnp.where(jnp.logical_and(begin < p.R, end > p.R), 1, after)
            return end, first, last, before, after, lowest, highest

        zero = jnp.int32(0)
        _, first, last, before, after, lowest, highest = lax.fori_loop(0, p.A, agg, (-here * p.R,) + (zero,) * 6)
        trims[0] = jnp.clip(first, 0, p.R)
        trims[1] = jnp.clip(last, 0, p.R)
        trims[2] = before
        trims[3] = after
        trims[4] = lowest
        trims[5] = highest

    ints = lambda n: jax.ShapeDtypeStruct((n,), I32)
    return pl.pallas_call(
        kernel,
        in_specs=[SMEM, VM, VM, SMEM] + [HBM] * 3 + [SMEM] + [ANY] * 4,
        out_specs=[VM] * 7 + [SMEM] * 6,
        out_shape=[
            pltpu.VMEM(rhs.shape, BF16),
            pltpu.VMEM(smoother.shape, BF16),
            pltpu.VMEM((2 * p.H,) + blocks.shape[1:], BF16),
            pltpu.VMEM((p.A, p.BS, p.BS), BF16),
            pltpu.VMEM((p.R, p.BS, p.N), F32),
            pltpu.VMEM((p.R + 1, p.BS, p.N), BF16),
            pltpu.VMEM((2 * p.H, p.BS, p.N), F32),
            *[jax.ShapeDtypeStruct((p.K, p.R), I32)] * 4,
            ints(p.A + 1),
            ints(6),
        ],
        scratch_shapes=[
            pltpu.VMEM((4, p.K, p.R), I32),
            pltpu.SemaphoreType.DMA((3, pieces)),
            pltpu.SemaphoreType.DMA((4,)),
            pltpu.SemaphoreType.DMA((p.G,)),
        ],
        compiler_params=params(8),
        cost_estimate=cost(2 * p.R * p.K * p.BS * p.BS * p.N, 2 * p.R * p.K * p.BS * p.BS),
        name="first_sweep",
    )(pos, cols, counts, sizes, far(rhs), far(smoother), far(blocks), apart, *inverses)


GROUP = 4
WIDE = 4


def halo_product(hslot, hcol, blk, r, i, slots, halo):
    lhs = jnp.concatenate([blk[r, hslot[j, i]] for j in slots], axis=1)
    rhs = jnp.concatenate([halo[hcol[j, i]] for j in slots], axis=0)
    return mm(lhs, rhs)


def take_rest(p, hslot, hcol, hn, blk, halo, acc, rows):
    def row(r, c):
        i = end_row(p, r)

        @pl.when(hn[0, i] > WIDE)
        def _():
            acc[r] = acc[r] - halo_product(hslot, hcol, blk, r, i, range(WIDE, p.K), halo)

        return c

    for first, last in rows:
        lax.fori_loop(first, last, row, 0)


def put_halo(p, odd, halo, from_odd, from_even, before, after):
    step = p.H // 2
    halo[pl.ds(jnp.where(odd > 0, after, before), step)] = from_odd[...]
    halo[pl.ds(jnp.where(odd > 0, before, after), step)] = from_even[...]


def edge_second(p, outer, pos, hslot, hcol, hn, parts, acc, smoother, blocks, s2, ext2=None, halo=None):
    step = p.H // 2
    halves = ((0, step), (2 * p.H - step, 2 * p.H)) if outer else ((step, p.H), (p.H, p.H + step))
    before, after = (0, 2 * p.H - step) if outer else (step, p.H)

    def kernel(pos_ref, hs, hc, hn_ref, acc_in, s2_in, *rest):
        from_odd, from_even, sm, blk = rest[-12:-8]
        acc_ref, s2_out, ext_out, halo_ref, to_odd, to_even, res, sent = rest[-8:]
        odd = pos_ref[2]
        put_halo(p, odd, halo_ref, from_odd, from_even, before, after)
        if not outer:
            halo_ref[2 * p.H] = jnp.zeros((p.BS, p.N), BF16)
            ext_out[p.R] = jnp.zeros((p.BS, p.N), BF16)
        take_rest(p, hs, hc, hn_ref, blk, halo_ref, acc_ref, halves)
        for first, last in halves:

            def residual(r, c):
                i = end_row(p, r)
                res[r] = (acc_ref[r] - halo_product(hs, hc, blk, r, i, range(WIDE), halo_ref)).astype(BF16)
                return c

            lax.fori_loop(first, last, residual, 0, unroll=8)
        for h, (first, last) in enumerate(halves):
            shift_by = 0 if first < p.H else p.R - 2 * p.H
            for g in range(first, last, GROUP):
                rows = range(g, g + GROUP)
                new = [s2_in[shift_by + r] + relax_fine * mm(sm[shift_by + r], res[r]) for r in rows]
                for r, v in zip(rows, new):
                    s2_out[shift_by + r] = v
                    sent[h, r - first] = v.astype(BF16)
                    ext_out[shift_by + r] = v.astype(BF16)
        to_odd[...] = sent[odd]
        to_even[...] = sent[1 - odd]

    out = jax.ShapeDtypeStruct((step, p.BS, p.N), BF16)
    kept = [] if not outer else [near(ext2), near(halo)]
    return pl.pallas_call(
        kernel,
        in_specs=[SMEM] * 4 + [VM] * (6 + len(kept)),
        out_specs=[VM] * 6,
        out_shape=[
            pltpu.VMEM((2 * p.H, p.BS, p.N), F32),
            pltpu.VMEM((p.R, p.BS, p.N), F32),
            pltpu.VMEM((p.R + 1, p.BS, p.N), BF16),
            pltpu.VMEM((2 * p.H + 1, p.BS, p.N), BF16),
            out,
            out,
        ],
        input_output_aliases={4: 0, 5: 1, **({6: 2, 7: 3} if outer else {})},
        scratch_shapes=[
            pltpu.VMEM((2 * p.H, p.BS, p.N), BF16),
            pltpu.VMEM((2, step, p.BS, p.N), BF16),
        ],
        compiler_params=params(8),
        cost_estimate=cost(8 * p.H * p.BS * p.BS * p.N, 4 * p.H * p.K * p.BS * p.BS),
        name="edge_second_outer" if outer else "edge_second_inner",
    )(
        pos, hslot, hcol, hn, near(acc), near(s2), *kept, near(parts[0]), near(parts[1]), near(smoother), near(blocks)
    )


def aggregate_sum(p, resid, first, last):
    return lax.fori_loop(
        first, last, lambda r, t: t + resid[r].astype(F32), jnp.zeros((p.BS, p.N), F32)
    )


def add_fix(inverse, res, s2, first, last):
    fix = (relax_coarse * mm(inverse, res)).astype(BF16).astype(F32)

    def row(r, c):
        s2[r] = s2[r] + fix
        return c

    lax.fori_loop(first, last, row, 0)


def inner_aggregate(p, first, last):
    return jnp.logical_and(first >= p.H, last <= p.R - p.H)


def inner_second(p, lcol, rhs, smoother, ext1, ext2, s2, blocks):
    piece = 4
    inner = p.R - 2 * p.H

    def kernel(lcol_ref, b, sm, ext1_ref, ext_in, s2_ref, blk_hbm, ext, s2_out, blk, blk_sems):
        def block_copy(c):
            src = blk_hbm.at[pl.ds(p.H + c * piece, piece)]
            return pltpu.make_async_copy(src, blk.at[pl.ds(c * piece, piece)], blk_sems.at[c])

        for c in range(inner // piece):
            block_copy(c).start()
        for c in range(inner // piece):
            block_copy(c).wait()
            rows = range(c * piece, (c + 1) * piece)
            res = [
                (b[p.H + r].astype(F32) - row_product(p, blk, r, p.H + r, ext1_ref, lcol_ref)).astype(BF16) for r in rows
            ]
            new = [s2_ref[p.H + r] + relax_fine * mm(sm[p.H + r], v) for r, v in zip(rows, res)]
            for r, v in zip(rows, new):
                s2_out[p.H + r] = v
                ext[p.H + r] = v.astype(BF16)

    return pl.pallas_call(
        kernel,
        in_specs=[SMEM] + [VM] * 5 + [HBM],
        out_specs=[VM] * 3,
        out_shape=[
            pltpu.VMEM((p.R + 1, p.BS, p.N), BF16),
            pltpu.VMEM((p.R, p.BS, p.N), F32),
            pltpu.VMEM((inner,) + blocks.shape[1:], BF16),
        ],
        input_output_aliases={4: 0, 5: 1},
        scratch_shapes=[pltpu.SemaphoreType.DMA((inner // piece,))],
        compiler_params=params(8),
        cost_estimate=cost(0, 0),
        name="inner_second",
    )(lcol, near(rhs), near(smoother), near(ext1), near(ext2), near(s2), far(blocks))


def inner_rows(p, pos, lcol, bounds, rhs, end_blocks, blocks, ext, s2, parts, inv):
    inner = p.R - 2 * p.H

    def kernel(
        pos_ref, lcol_ref, bd, b, end_blk, blk, ext, inv, s2_ref, from_odd, from_even,
        r2, acc, s2_out, halo, out, row_sems,
    ):
        put_halo(p, pos_ref[2], halo, from_odd, from_even, 0, 2 * p.H - p.H // 2)

        def inner_row(r, c):
            i = p.H + r
            r2[i] = (b[i].astype(F32) - row_product(p, blk, r, i, ext, lcol_ref)).astype(BF16)
            return c

        lax.fori_loop(0, inner, inner_row, 0, unroll=4)

        def copy(r):
            return pltpu.make_async_copy(s2_out.at[r], out.at[r], row_sems.at[r])

        def send(r, c):
            copy(r).start()
            return c

        def wait(r, c):
            copy(r).wait()
            return c

        def aggregates(act):
            def one(a, c):
                first, last = bd[a], bd[a + 1]
                pl.when(jnp.logical_and(first < last, inner_aggregate(p, first, last)))(lambda: act(a, first, last))
                return c

            lax.fori_loop(0, p.A, one, 0)

        def fix(a, first, last):
            res = aggregate_sum(p, r2, first, last).astype(BF16)
            add_fix(inv[a], res, s2_out, first, last)
            lax.fori_loop(first, last, send, 0)

        aggregates(fix)

        def edge_row(r, c):
            i = end_row(p, r)
            acc[r] = b[i].astype(F32) - row_product(p, end_blk, r, i, ext, lcol_ref)
            return c

        lax.fori_loop(0, 2 * p.H, edge_row, 0, unroll=4)

        def settle(a, first, last):
            lax.fori_loop(first, last, wait, 0)

        aggregates(settle)

    return pl.pallas_call(
        kernel,
        in_specs=[SMEM] * 3 + [VM] * 8,
        out_specs=[VM] * 4 + [HBM],
        out_shape=[
            pltpu.VMEM((p.R, p.BS, p.N), BF16),
            pltpu.VMEM((2 * p.H, p.BS, p.N), F32),
            pltpu.VMEM((p.R, p.BS, p.N), F32),
            pltpu.VMEM((2 * p.H + 1, p.BS, p.N), BF16),
            jax.ShapeDtypeStruct((p.R, p.BS, p.N), F32),
        ],
        input_output_aliases={8: 2},
        scratch_shapes=[pltpu.SemaphoreType.DMA((p.R,))],
        compiler_params=params(8),
        cost_estimate=cost(4 * p.R * p.K * p.BS * p.BS * p.N, p.R * p.K * p.BS * p.BS),
        name="inner_rows",
    )(
        pos, lcol, bounds, near(rhs), near(end_blocks), near(blocks), near(ext), near(inv), near(s2), *map(near, parts)
    )


def edge_final(p, pos, hslot, hcol, hn, trims, parts, halo, acc, blocks, r2):
    step = p.H // 2

    def kernel(pos_ref, hs, hc, hn_ref, trim, from_odd, from_even, halo_in, acc_in, blk, r2_in, *rest):
        r2_out, acc_ref, halo, part_first, part_last, to_odd, to_even, both = rest
        put_halo(p, pos_ref[2], halo, from_odd, from_even, step, p.H)
        halo[2 * p.H] = jnp.zeros((p.BS, p.N), BF16)
        take_rest(p, hs, hc, hn_ref, blk, halo, acc_ref, ((0, 2 * p.H),))

        def row(r, c):
            i = end_row(p, r)
            r2_out[i] = (acc_ref[r] - halo_product(hs, hc, blk, r, i, range(WIDE), halo)).astype(BF16)
            return c

        lax.fori_loop(0, 2 * p.H, row, 0, unroll=8)
        both[0] = aggregate_sum(p, r2_out, 0, trim[0]).astype(BF16)
        both[1] = aggregate_sum(p, r2_out, trim[1], p.R).astype(BF16)
        part_first[...] = both[0]
        part_last[...] = both[1]
        odd = pos_ref[1] & 1
        to_odd[...] = both[odd]
        to_even[...] = both[1 - odd]

    one = jax.ShapeDtypeStruct((p.BS, p.N), BF16)
    return pl.pallas_call(
        kernel,
        in_specs=[SMEM] * 5 + [VM] * 6,
        out_specs=[VM] * 7,
        out_shape=[
            pltpu.VMEM((p.R, p.BS, p.N), BF16),
            pltpu.VMEM((2 * p.H, p.BS, p.N), F32),
            pltpu.VMEM((2 * p.H + 1, p.BS, p.N), BF16),
            *[one] * 4,
        ],
        input_output_aliases={10: 0, 8: 1, 7: 2},
        scratch_shapes=[pltpu.VMEM((2, p.BS, p.N), BF16)],
        compiler_params=params(8),
        cost_estimate=cost(4 * p.H * p.BS * p.BS * p.N, 4 * p.H * p.K * p.BS * p.BS),
        name="edge_final",
    )(pos, hslot, hcol, hn, trims, *map(near, parts), near(halo), near(acc), near(blocks), near(r2))


def coarse_own(p, bounds, trims, r2, s2, inv):
    def kernel(bd, trim, r2_ref, s2_in, inv_ref, s2_ref):
        def one(a, c):
            first, last = bd[a], bd[a + 1]
            split = jnp.logical_or(
                jnp.logical_and(first == 0, trim[2] > 0), jnp.logical_and(last == p.R, trim[3] > 0)
            )
            done = jnp.logical_or(split, inner_aggregate(p, first, last))

            @pl.when(jnp.logical_and(first < last, jnp.logical_not(done)))
            def _():
                res = aggregate_sum(p, r2_ref, first, last).astype(BF16)
                add_fix(inv_ref[a], res, s2_ref, first, last)

            return c

        lax.fori_loop(0, p.A, one, 0)

    return pl.pallas_call(
        kernel,
        in_specs=[SMEM] * 2 + [VM] * 3,
        out_specs=VM,
        out_shape=pltpu.VMEM((p.R, p.BS, p.N), F32),
        input_output_aliases={3: 0},
        compiler_params=params(8),
        cost_estimate=cost(p.A * p.BS * p.BS * p.N, 5 * p.R * p.BS * p.N),
        name="coarse_own",
    )(bounds, trims, near(r2), near(s2), near(inv))


def coarse_split(p, pos, bounds, trims, part_first, part_last, parts, s2, inv, out):
    def kernel(
        pos_ref, bd, trim, first_ref, last_ref, by_odd, by_even, s2_in, inv_ref, out_in, s2_ref, out_ref, row_sems
    ):
        odd = (pos_ref[1] & 1) > 0
        bef = jnp.where(odd, by_even[...].astype(F32), by_odd[...].astype(F32))
        aft = jnp.where(odd, by_odd[...].astype(F32), by_even[...].astype(F32))

        @pl.when(trim[2] > 0)
        def _():
            res = (bef + first_ref[...].astype(F32)).astype(BF16)
            add_fix(inv_ref[trim[4]], res, s2_ref, 0, trim[0])

        @pl.when(trim[3] > 0)
        def _():
            res = (last_ref[...].astype(F32) + aft).astype(BF16)
            add_fix(inv_ref[trim[5]], res, s2_ref, trim[1], p.R)

        def inner(a, t):
            begin, end = t
            first, last = bd[a], bd[a + 1]
            sent = jnp.logical_and(first < last, inner_aggregate(p, first, last))
            return jnp.where(sent, jnp.minimum(begin, first), begin), jnp.where(sent, last, end)

        begin, end = lax.fori_loop(0, p.A, inner, (jnp.int32(p.R), jnp.int32(p.R)))

        def copy(r):
            return pltpu.make_async_copy(s2_ref.at[r], out_ref.at[r], row_sems.at[r])

        def send(r, c):
            copy(r).start()
            return c

        def wait(r, c):
            copy(r).wait()
            return c

        for step in (send, wait):
            lax.fori_loop(0, begin, step, 0)
            lax.fori_loop(end, p.R, step, 0)

    return pl.pallas_call(
        kernel,
        in_specs=[SMEM] * 3 + [VM] * 6 + [HBM],
        out_specs=[VM, HBM],
        out_shape=[
            pltpu.VMEM((p.R, p.BS, p.N), F32),
            jax.ShapeDtypeStruct((p.R, p.BS, p.N), F32),
        ],
        input_output_aliases={7: 0, 9: 1},
        scratch_shapes=[pltpu.SemaphoreType.DMA((p.R,))],
        compiler_params=params(8),
        cost_estimate=cost(4 * p.BS * p.BS * p.N, p.R * p.BS * p.N),
        name="coarse_split",
    )(
        pos, bounds, trims, near(part_first), near(part_last), *map(near, parts), near(s2), near(inv), out
    )[1]


def swaps(axis, odd):
    size = lax.axis_size(axis)
    pairs = [(i, i + 1) for i in range(odd, size - 1, 2)]
    return lambda value: lax.ppermute(value, axis, pairs + [(j, i) for i, j in pairs])


def body(load_rhs, blocks, columns, counts, smoother, agg_sizes, coarse_inv):
    rows, bs, n = load_rhs.shape
    group = lax.axis_size("agg")
    p = Sizes(rows, blocks.shape[1], bs, n, agg_sizes.shape[1], group)
    here = lax.axis_index("agg")
    index = lax.axis_index(AXES)
    pos = jnp.stack([index * rows, here, index & 1]).astype(I32)

    swap_odd, swap_even = swaps(AXES, 1), swaps(AXES, 0)

    apart, *out1 = edge_smooth(p, pos, agg_sizes, load_rhs, smoother)
    inner1 = swap_odd(out1[0]), swap_even(out1[1])
    outer1 = swap_odd(out1[2]), swap_even(out1[3])

    def every(own):
        turn = lambda t: lax.ppermute(own, "agg", [(i, (i + t) % group) for i in range(group)])
        return jnp.stack([turn(t) for t in range(1, group)])

    def none(own):
        return jnp.zeros((group - 1,) + own.shape, own.dtype)

    distant = lax.cond(apart[0] > 1, every, none, coarse_inv)
    inverses = coarse_inv, swaps("agg", 1)(coarse_inv), swaps("agg", 0)(coarse_inv), distant
    rhs, smoother, end_blocks, inv, s2, ext1, acc1, lcol, hslot, hcol, hn, bounds, trims = first_sweep(
        p, pos, columns.T, counts[None, :], agg_sizes, load_rhs, smoother, blocks, apart, inverses
    )
    acc1, s2, ext2, halo, *out2 = edge_second(
        p, False, pos, hslot, hcol, hn, inner1, acc1, smoother, end_blocks, s2
    )
    inner2 = swap_odd(out2[0]), swap_even(out2[1])
    _, s2, ext2, _, *out2 = edge_second(
        p, True, pos, hslot, hcol, hn, outer1, acc1, smoother, end_blocks, s2, ext2, halo
    )
    outer2 = swap_odd(out2[0]), swap_even(out2[1])
    ext2, s2, inner_blocks = inner_second(p, lcol, rhs, smoother, ext1, ext2, s2, blocks)
    r2, acc2, s2, halo, out = inner_rows(
        p, pos, lcol, bounds, rhs, end_blocks, inner_blocks, ext2, s2, inner2, inv
    )
    r2, _, _, part_first, part_last, to_odd, to_even = edge_final(
        p, pos, hslot, hcol, hn, trims, outer2, halo, acc2, end_blocks, r2
    )
    parts = swaps("agg", 1)(to_odd), swaps("agg", 0)(to_even)
    s2 = coarse_own(p, bounds, trims, r2, s2, inv)
    return coarse_split(p, pos, bounds, trims, part_first, part_last, parts, s2, inv, out)


def solution(mesh):
    placed = (
        P(AXES, None, None),
        P(AXES, None, None, None),
        P(AXES, None),
        P(AXES),
        P(AXES, None, None),
        P("rows", None),
        P(AXES, None, None),
    )
    return jax.shard_map(
        body, mesh=mesh, in_specs=placed, out_specs=P(AXES, None, None), check_vma=False
    )
```

```python
import jax
import jax.numpy as jnp
from jax import lax
from jax.experimental import pallas as pl
from jax.experimental.pallas import tpu as pltpu
from jax.sharding import PartitionSpec as P

HALO = 16

relax_fine = 0.8
relax_coarse = 1.0

AXES = ("rows", "agg")
F32 = jnp.float32
BF16 = jnp.bfloat16
I32 = jnp.int32
MIB = 1024 * 1024
WEIGHT = 32

SMEM = pl.BlockSpec(memory_space=pltpu.SMEM)
VM = pl.BlockSpec(memory_space=pltpu.VMEM)
ANY = pl.BlockSpec(memory_space=pl.ANY)
HBM = pl.BlockSpec(memory_space=pltpu.HBM)


def mm(a, b):
    return jnp.dot(a, b, preferred_element_type=F32)


def cost(flops, nbytes):
    return pl.CostEstimate(flops=WEIGHT * flops, bytes_accessed=nbytes, transcendentals=0)


def params(mib):
    return pltpu.CompilerParams(vmem_limit_bytes=mib * MIB)


def near(x):
    return pltpu.with_memory_space_constraint(x, pltpu.VMEM)


def far(x):
    return pltpu.with_memory_space_constraint(x, pltpu.HBM)


class Sizes:
    def __init__(self, rows, slots, bs, n, aggs, group):
        self.R, self.K, self.BS, self.N, self.A, self.G = rows, slots, bs, n, aggs, group
        self.H = HALO


def edge_smooth(p, pos, rhs, smoother):
    step = p.H // 2

    def kernel(pos_ref, b_hbm, s_hbm, *rest):
        outs, (b, s, sems) = rest[:4], rest[4:]
        odd = pos_ref[2]
        starts = []
        for first, last in ((0, p.R - step), (step, p.R - 2 * step)):
            starts += [jnp.where(odd > 0, last, first), jnp.where(odd > 0, first, last)]
        copies = []
        for c, at in enumerate(starts):
            copies.append(pltpu.make_async_copy(b_hbm.at[pl.ds(at, step)], b.at[c], sems.at[0, c]))
            copies.append(pltpu.make_async_copy(s_hbm.at[pl.ds(at, step)], s.at[c], sems.at[1, c]))
        for c in copies:
            c.start()

        for c in range(4):
            copies[2 * c].wait()
            copies[2 * c + 1].wait()
            for r in range(step):
                outs[c][r] = (relax_fine * mm(s[c, r], b[c, r])).astype(BF16)

    out = jax.ShapeDtypeStruct((step, p.BS, p.N), BF16)
    return pl.pallas_call(
        kernel,
        in_specs=[SMEM, HBM, HBM],
        out_specs=[VM] * 4,
        out_shape=[out] * 4,
        scratch_shapes=[
            pltpu.VMEM((4, step, p.BS, p.N), BF16),
            pltpu.VMEM((4, step, p.BS, p.BS), BF16),
            pltpu.SemaphoreType.DMA((2, 4)),
        ],
        compiler_params=params(8),
        cost_estimate=cost(4 * p.H * p.BS * p.BS * p.N, 6 * p.H * p.BS * p.N),
        name="edge_smooth",
    )(pos, far(rhs), far(smoother))


def end_row(p, r):
    return jnp.where(r < p.H, r, r + p.R - 2 * p.H)


def row_product(p, blk, at, i, ext, lcol):
    lhs = jnp.concatenate([blk[at, k] for k in range(p.K)], axis=1)
    rhs = jnp.concatenate([ext[lcol[k, i]] for k in range(p.K)], axis=0)
    return mm(lhs, rhs)


def first_sweep(p, pos, cols, counts, sizes, rhs, smoother, blocks, apart, inverses):
    piece = p.H // 2
    share = p.A // p.G
    pieces = p.R // piece
    end_pieces = 2 * p.H // piece

    def kernel(
        pos_ref, col_ref, cnt_ref, size_ref, b_hbm, sm_hbm, blk_hbm, apart_ref, own, by_odd, by_even, distant,
        b, sm, blk, inv, s2, ext, acc, lcol, hslot, hcol, hn, bounds, trims, lists, sems, list_sems, inv_sems,
    ):
        start, here = pos_ref[0], pos_ref[1]
        small = [
            pltpu.make_async_copy(src.at[pl.ds(c * piece, piece)], dst.at[pl.ds(c * piece, piece)], sems.at[j, c])
            for c in range(pieces)
            for j, (src, dst) in enumerate(((b_hbm, b), (sm_hbm, sm)))
        ]

        def block_copy(c):
            src = pl.ds(c * piece if c < end_pieces // 2 else p.R - 2 * p.H + c * piece, piece)
            return pltpu.make_async_copy(blk_hbm.at[src], blk.at[pl.ds(c * piece, piece)], sems.at[2, c])

        for c in small:
            c.start()
        for c in range(end_pieces):
            block_copy(c).start()
        back = jnp.where((pos_ref[1] & 1) > 0, p.G - 1, 1)

        def inverse_copy(src, distance, t):
            at = pl.ds(lax.rem(pos_ref[1] - distance + p.G, p.G) * share, share)
            return pltpu.make_async_copy(src, inv.at[at], inv_sems.at[t])

        def place_all(act):
            act(inverse_copy(own, 0, 0))

            @pl.when(apart_ref[0] <= 1)
            def _():
                act(inverse_copy(by_odd, back, 1))
                act(inverse_copy(by_even, p.G - back, 2))

            @pl.when(apart_ref[0] > 1)
            def _():
                for t in range(1, p.G):
                    act(inverse_copy(distant.at[t - 1], t, t))

        place_all(lambda c: c.start())
        ext[p.R] = jnp.zeros((p.BS, p.N), BF16)

        cols = col_ref[...] - start
        ks = lax.broadcasted_iota(I32, (p.K, p.R), 0)
        live = ks < cnt_ref[...]
        inside = jnp.logical_and(cols >= 0, cols < p.R)
        lists[0] = jnp.where(jnp.logical_and(live, inside), cols, p.R)
        outside = jnp.where(jnp.logical_and(live, jnp.logical_not(inside)), 1, 0)
        place = jnp.where(cols < 0, cols + p.H, cols - p.R + p.H)
        count = jnp.zeros((1, p.R), I32)
        slot_rows = [jnp.zeros((1, p.R), I32)] * p.K
        col_rows = [jnp.full((1, p.R), 2 * p.H, I32)] * p.K
        for k in range(p.K):
            out = outside[k:k + 1]
            for j in range(k + 1):
                mine = jnp.logical_and(out > 0, count == j)
                slot_rows[j] = jnp.where(mine, k, slot_rows[j])
                col_rows[j] = jnp.where(mine, place[k:k + 1], col_rows[j])
            count = count + out
        lists[1] = jnp.concatenate(slot_rows, axis=0)
        lists[2] = jnp.concatenate(col_rows, axis=0)
        lists[3] = jnp.broadcast_to(count, (p.K, p.R))
        list_copies = [
            pltpu.make_async_copy(lists.at[j], dst, list_sems.at[j]) for j, dst in enumerate((lcol, hslot, hcol, hn))
        ]
        for c in list_copies:
            c.start()

        def smooth_row(r, c):
            v = relax_fine * mm(sm[r], b[r])
            s2[r] = v
            ext[r] = v.astype(BF16)
            return c

        for c in range(pieces):
            small[2 * c].wait()
            small[2 * c + 1].wait()
            lax.fori_loop(c * piece, (c + 1) * piece, smooth_row, 0, unroll=8)

        for c in list_copies:
            c.wait()

        def edge_row(r, c):
            i = end_row(p, r)
            acc[r] = b[i].astype(F32) - row_product(p, blk, r, i, ext, lcol)
            return c

        for c in range(end_pieces):
            block_copy(c).wait()
            if c not in (0, end_pieces - 1):
                lax.fori_loop(c * piece, (c + 1) * piece, edge_row, 0, unroll=8)

        place_all(lambda c: c.wait())

        bounds[0] = 0

        def agg(a, t):
            end, first, last, before, after, lowest, highest = t
            begin = end
            end = end + size_ref[0, a]
            bounds[a + 1] = jnp.clip(end, 0, p.R)
            leads = jnp.logical_and(begin <= 0, end > 0)
            ends = jnp.logical_and(begin < p.R, end >= p.R)
            first = jnp.where(leads, end, first)
            last = jnp.where(ends, begin, last)
            lowest = jnp.where(leads, a, lowest)
            highest = jnp.where(ends, a, highest)
            before = jnp.where(jnp.logical_and(begin < 0, end > 0), 1, before)
            after = jnp.where(jnp.logical_and(begin < p.R, end > p.R), 1, after)
            return end, first, last, before, after, lowest, highest

        zero = jnp.int32(0)
        _, first, last, before, after, lowest, highest = lax.fori_loop(0, p.A, agg, (-here * p.R,) + (zero,) * 6)
        trims[0] = jnp.clip(first, 0, p.R)
        trims[1] = jnp.clip(last, 0, p.R)
        trims[2] = before
        trims[3] = after
        trims[4] = lowest
        trims[5] = highest

    ints = lambda n: jax.ShapeDtypeStruct((n,), I32)
    return pl.pallas_call(
        kernel,
        in_specs=[SMEM, VM, VM, SMEM] + [HBM] * 3 + [SMEM] + [ANY] * 4,
        out_specs=[VM] * 7 + [SMEM] * 6,
        out_shape=[
            pltpu.VMEM(rhs.shape, BF16),
            pltpu.VMEM(smoother.shape, BF16),
            pltpu.VMEM((2 * p.H,) + blocks.shape[1:], BF16),
            pltpu.VMEM((p.A, p.BS, p.BS), BF16),
            pltpu.VMEM((p.R, p.BS, p.N), F32),
            pltpu.VMEM((p.R + 1, p.BS, p.N), BF16),
            pltpu.VMEM((2 * p.H, p.BS, p.N), F32),
            *[jax.ShapeDtypeStruct((p.K, p.R), I32)] * 4,
            ints(p.A + 1),
            ints(6),
        ],
        scratch_shapes=[
            pltpu.VMEM((4, p.K, p.R), I32),
            pltpu.SemaphoreType.DMA((3, pieces)),
            pltpu.SemaphoreType.DMA((4,)),
            pltpu.SemaphoreType.DMA((p.G,)),
        ],
        compiler_params=params(8),
        cost_estimate=cost(2 * p.R * p.K * p.BS * p.BS * p.N, 2 * p.R * p.K * p.BS * p.BS),
        name="first_sweep",
    )(pos, cols, counts, sizes, far(rhs), far(smoother), far(blocks), apart, *inverses)


GROUP = 4
NARROW, WIDE = 4, 6


def outer_local(p, lcol, rhs, blocks, ext, acc):
    step = p.H // 2

    def kernel(lcol_ref, b, blk, ext_ref, acc_in, acc_ref):
        def edge_row(r, c):
            i = end_row(p, r)
            acc_ref[r] = b[i].astype(F32) - row_product(p, blk, r, i, ext_ref, lcol_ref)
            return c

        lax.fori_loop(0, step, edge_row, 0, unroll=8)
        lax.fori_loop(2 * p.H - step, 2 * p.H, edge_row, 0, unroll=8)

    return pl.pallas_call(
        kernel,
        in_specs=[SMEM] + [VM] * 4,
        out_specs=VM,
        out_shape=pltpu.VMEM((2 * p.H, p.BS, p.N), F32),
        input_output_aliases={4: 0},
        compiler_params=params(8),
        cost_estimate=cost(0, 0),
        name="outer_local",
    )(lcol, near(rhs), near(blocks), near(ext), near(acc))


def halo_product(hslot, hcol, blk, r, i, slots, halo):
    lhs = jnp.concatenate([blk[r, hslot[j, i]] for j in slots], axis=1)
    rhs = jnp.concatenate([halo[hcol[j, i]] for j in slots], axis=0)
    return mm(lhs, rhs)


def take_rest(p, hslot, hcol, hn, blk, halo, acc, rows, taken):
    def row(r, c):
        i = end_row(p, r)

        @pl.when(hn[0, i] > taken)
        def _():
            acc[r] = acc[r] - halo_product(hslot, hcol, blk, r, i, range(taken, p.K), halo)

        return c

    for first, last in rows:
        lax.fori_loop(first, last, row, 0)


def put_halo(p, odd, halo, from_odd, from_even, before, after):
    step = p.H // 2
    halo[pl.ds(jnp.where(odd > 0, after, before), step)] = from_odd[...]
    halo[pl.ds(jnp.where(odd > 0, before, after), step)] = from_even[...]


def edge_second(p, outer, pos, hslot, hcol, hn, parts, acc, smoother, blocks, s2, ext2=None, halo=None):
    step = p.H // 2
    halves = ((0, step), (2 * p.H - step, 2 * p.H)) if outer else ((step, p.H), (p.H, p.H + step))
    before, after = (0, 2 * p.H - step) if outer else (step, p.H)
    taken = min(p.K, WIDE if outer else NARROW)

    def kernel(pos_ref, hs, hc, hn_ref, acc_in, s2_in, *rest):
        from_odd, from_even, sm, blk = rest[-12:-8]
        acc_ref, s2_out, ext_out, halo_ref, to_odd, to_even, res, sent = rest[-8:]
        odd = pos_ref[2]
        put_halo(p, odd, halo_ref, from_odd, from_even, before, after)
        if not outer:
            halo_ref[2 * p.H] = jnp.zeros((p.BS, p.N), BF16)
            ext_out[p.R] = jnp.zeros((p.BS, p.N), BF16)
        take_rest(p, hs, hc, hn_ref, blk, halo_ref, acc_ref, halves, taken)
        for first, last in halves:

            def residual(r, c):
                i = end_row(p, r)
                res[r] = (acc_ref[r] - halo_product(hs, hc, blk, r, i, range(taken), halo_ref)).astype(BF16)
                return c

            lax.fori_loop(first, last, residual, 0, unroll=8)
        for h, (first, last) in enumerate(halves):
            shift_by = 0 if first < p.H else p.R - 2 * p.H
            for g in range(first, last, GROUP):
                rows = range(g, g + GROUP)
                new = [s2_in[shift_by + r] + relax_fine * mm(sm[shift_by + r], res[r]) for r in rows]
                for r, v in zip(rows, new):
                    s2_out[shift_by + r] = v
                    sent[h, r - first] = v.astype(BF16)
                    ext_out[shift_by + r] = v.astype(BF16)
        to_odd[...] = sent[odd]
        to_even[...] = sent[1 - odd]

    out = jax.ShapeDtypeStruct((step, p.BS, p.N), BF16)
    kept = [] if not outer else [near(ext2), near(halo)]
    return pl.pallas_call(
        kernel,
        in_specs=[SMEM] * 4 + [VM] * (6 + len(kept)),
        out_specs=[VM] * 6,
        out_shape=[
            pltpu.VMEM((2 * p.H, p.BS, p.N), F32),
            pltpu.VMEM((p.R, p.BS, p.N), F32),
            pltpu.VMEM((p.R + 1, p.BS, p.N), BF16),
            pltpu.VMEM((2 * p.H + 1, p.BS, p.N), BF16),
            out,
            out,
        ],
        input_output_aliases={4: 0, 5: 1, **({6: 2, 7: 3} if outer else {})},
        scratch_shapes=[
            pltpu.VMEM((2 * p.H, p.BS, p.N), BF16),
            pltpu.VMEM((2, step, p.BS, p.N), BF16),
        ],
        compiler_params=params(8),
        cost_estimate=cost(8 * p.H * p.BS * p.BS * p.N, 4 * p.H * p.K * p.BS * p.BS),
        name="edge_second_outer" if outer else "edge_second_inner",
    )(
        pos, hslot, hcol, hn, near(acc), near(s2), *kept, near(parts[0]), near(parts[1]), near(smoother), near(blocks)
    )


def aggregate_sum(p, resid, first, last):
    return lax.fori_loop(
        first, last, lambda r, t: t + resid[r].astype(F32), jnp.zeros((p.BS, p.N), F32)
    )


def add_fix(inverse, res, s2, first, last):
    fix = (relax_coarse * mm(inverse, res)).astype(BF16).astype(F32)

    def row(r, c):
        s2[r] = s2[r] + fix
        return c

    lax.fori_loop(first, last, row, 0)


def inner_aggregate(p, first, last):
    return jnp.logical_and(first >= p.H, last <= p.R - p.H)


def inner_second(p, lcol, rhs, smoother, ext1, ext2, s2, blocks):
    piece = 8
    inner = p.R - 2 * p.H

    def kernel(lcol_ref, b, sm, ext1_ref, ext_in, s2_ref, blk_hbm, ext, s2_out, blk, blk_sems):
        def block_copy(c):
            src = blk_hbm.at[pl.ds(p.H + c * piece, piece)]
            return pltpu.make_async_copy(src, blk.at[pl.ds(c * piece, piece)], blk_sems.at[c])

        for c in range(inner // piece):
            block_copy(c).start()
        for c in range(inner // piece):
            block_copy(c).wait()
            rows = range(c * piece, (c + 1) * piece)
            res = [
                (b[p.H + r].astype(F32) - row_product(p, blk, r, p.H + r, ext1_ref, lcol_ref)).astype(BF16) for r in rows
            ]
            new = [s2_ref[p.H + r] + relax_fine * mm(sm[p.H + r], v) for r, v in zip(rows, res)]
            for r, v in zip(rows, new):
                s2_out[p.H + r] = v
                ext[p.H + r] = v.astype(BF16)

    return pl.pallas_call(
        kernel,
        in_specs=[SMEM] + [VM] * 5 + [HBM],
        out_specs=[VM] * 3,
        out_shape=[
            pltpu.VMEM((p.R + 1, p.BS, p.N), BF16),
            pltpu.VMEM((p.R, p.BS, p.N), F32),
            pltpu.VMEM((inner,) + blocks.shape[1:], BF16),
        ],
        input_output_aliases={4: 0, 5: 1},
        scratch_shapes=[pltpu.SemaphoreType.DMA((inner // piece,))],
        compiler_params=params(8),
        cost_estimate=cost(0, 0),
        name="inner_second",
    )(lcol, near(rhs), near(smoother), near(ext1), near(ext2), near(s2), far(blocks))


def inner_rows(p, pos, lcol, bounds, rhs, end_blocks, blocks, ext, s2, parts, inv):
    inner = p.R - 2 * p.H

    def kernel(
        pos_ref, lcol_ref, bd, b, end_blk, blk, ext, inv, s2_ref, from_odd, from_even,
        r2, acc, s2_out, halo, out, row_sems,
    ):
        put_halo(p, pos_ref[2], halo, from_odd, from_even, 0, 2 * p.H - p.H // 2)

        def inner_row(r, c):
            i = p.H + r
            r2[i] = (b[i].astype(F32) - row_product(p, blk, r, i, ext, lcol_ref)).astype(BF16)
            return c

        lax.fori_loop(0, inner, inner_row, 0, unroll=8)

        def copy(r):
            return pltpu.make_async_copy(s2_out.at[r], out.at[r], row_sems.at[r])

        def send(r, c):
            copy(r).start()
            return c

        def wait(r, c):
            copy(r).wait()
            return c

        def aggregates(act):
            def one(a, c):
                first, last = bd[a], bd[a + 1]
                pl.when(jnp.logical_and(first < last, inner_aggregate(p, first, last)))(lambda: act(a, first, last))
                return c

            lax.fori_loop(0, p.A, one, 0)

        def fix(a, first, last):
            res = aggregate_sum(p, r2, first, last).astype(BF16)
            add_fix(inv[a], res, s2_out, first, last)
            lax.fori_loop(first, last, send, 0)

        aggregates(fix)

        def edge_row(r, c):
            i = end_row(p, r)
            acc[r] = b[i].astype(F32) - row_product(p, end_blk, r, i, ext, lcol_ref)
            return c

        lax.fori_loop(0, 2 * p.H, edge_row, 0, unroll=8)

        def settle(a, first, last):
            lax.fori_loop(first, last, wait, 0)

        aggregates(settle)

    return pl.pallas_call(
        kernel,
        in_specs=[SMEM] * 3 + [VM] * 8,
        out_specs=[VM] * 4 + [HBM],
        out_shape=[
            pltpu.VMEM((p.R, p.BS, p.N), BF16),
            pltpu.VMEM((2 * p.H, p.BS, p.N), F32),
            pltpu.VMEM((p.R, p.BS, p.N), F32),
            pltpu.VMEM((2 * p.H + 1, p.BS, p.N), BF16),
            jax.ShapeDtypeStruct((p.R, p.BS, p.N), F32),
        ],
        input_output_aliases={8: 2},
        scratch_shapes=[pltpu.SemaphoreType.DMA((p.R,))],
        compiler_params=params(8),
        cost_estimate=cost(4 * p.R * p.K * p.BS * p.BS * p.N, p.R * p.K * p.BS * p.BS),
        name="inner_rows",
    )(
        pos, lcol, bounds, near(rhs), near(end_blocks), near(blocks), near(ext), near(inv), near(s2), *map(near, parts)
    )


def edge_final(p, pos, hslot, hcol, hn, trims, parts, halo, acc, blocks, r2):
    step = p.H // 2

    def kernel(pos_ref, hs, hc, hn_ref, trim, from_odd, from_even, halo_in, acc_in, blk, r2_in, *rest):
        r2_out, acc_ref, halo, part_first, part_last, to_odd, to_even, both = rest
        put_halo(p, pos_ref[2], halo, from_odd, from_even, step, p.H)
        halo[2 * p.H] = jnp.zeros((p.BS, p.N), BF16)
        inner = ((step, 2 * p.H - step),)
        outer = ((0, step), (2 * p.H - step, 2 * p.H))
        for rows, taken in ((inner, min(p.K, NARROW)), (outer, min(p.K, WIDE))):
            take_rest(p, hs, hc, hn_ref, blk, halo, acc_ref, rows, taken)
            for first, last in rows:

                def row(r, c):
                    i = end_row(p, r)
                    r2_out[i] = (acc_ref[r] - halo_product(hs, hc, blk, r, i, range(taken), halo)).astype(BF16)
                    return c

                lax.fori_loop(first, last, row, 0, unroll=8)
        both[0] = aggregate_sum(p, r2_out, 0, trim[0]).astype(BF16)
        both[1] = aggregate_sum(p, r2_out, trim[1], p.R).astype(BF16)
        part_first[...] = both[0]
        part_last[...] = both[1]
        odd = pos_ref[1] & 1
        to_odd[...] = both[odd]
        to_even[...] = both[1 - odd]

    one = jax.ShapeDtypeStruct((p.BS, p.N), BF16)
    return pl.pallas_call(
        kernel,
        in_specs=[SMEM] * 5 + [VM] * 6,
        out_specs=[VM] * 7,
        out_shape=[
            pltpu.VMEM((p.R, p.BS, p.N), BF16),
            pltpu.VMEM((2 * p.H, p.BS, p.N), F32),
            pltpu.VMEM((2 * p.H + 1, p.BS, p.N), BF16),
            *[one] * 4,
        ],
        input_output_aliases={10: 0, 8: 1, 7: 2},
        scratch_shapes=[pltpu.VMEM((2, p.BS, p.N), BF16)],
        compiler_params=params(8),
        cost_estimate=cost(4 * p.H * p.BS * p.BS * p.N, 4 * p.H * p.K * p.BS * p.BS),
        name="edge_final",
    )(pos, hslot, hcol, hn, trims, *map(near, parts), near(halo), near(acc), near(blocks), near(r2))


def coarse_own(p, bounds, trims, r2, s2, inv):
    def kernel(bd, trim, r2_ref, s2_in, inv_ref, s2_ref):
        def one(a, c):
            first, last = bd[a], bd[a + 1]
            split = jnp.logical_or(
                jnp.logical_and(first == 0, trim[2] > 0), jnp.logical_and(last == p.R, trim[3] > 0)
            )
            done = jnp.logical_or(split, inner_aggregate(p, first, last))

            @pl.when(jnp.logical_and(first < last, jnp.logical_not(done)))
            def _():
                res = aggregate_sum(p, r2_ref, first, last).astype(BF16)
                add_fix(inv_ref[a], res, s2_ref, first, last)

            return c

        lax.fori_loop(0, p.A, one, 0)

    return pl.pallas_call(
        kernel,
        in_specs=[SMEM] * 2 + [VM] * 3,
        out_specs=VM,
        out_shape=pltpu.VMEM((p.R, p.BS, p.N), F32),
        input_output_aliases={3: 0},
        compiler_params=params(8),
        cost_estimate=cost(p.A * p.BS * p.BS * p.N, 5 * p.R * p.BS * p.N),
        name="coarse_own",
    )(bounds, trims, near(r2), near(s2), near(inv))


def coarse_split(p, pos, bounds, trims, part_first, part_last, parts, s2, inv, out):
    def kernel(
        pos_ref, bd, trim, first_ref, last_ref, by_odd, by_even, s2_in, inv_ref, out_in, s2_ref, out_ref, row_sems
    ):
        odd = (pos_ref[1] & 1) > 0
        bef = jnp.where(odd, by_even[...].astype(F32), by_odd[...].astype(F32))
        aft = jnp.where(odd, by_odd[...].astype(F32), by_even[...].astype(F32))

        def inner(a, t):
            begin, end = t
            first, last = bd[a], bd[a + 1]
            sent = jnp.logical_and(first < last, inner_aggregate(p, first, last))
            return jnp.where(sent, jnp.minimum(begin, first), begin), jnp.where(sent, last, end)

        begin, end = lax.fori_loop(0, p.A, inner, (jnp.int32(p.R), jnp.int32(p.R)))
        head = jnp.where(trim[2] > 0, trim[0], 0)
        tail = jnp.where(trim[3] > 0, trim[1], p.R)

        def copy(r):
            return pltpu.make_async_copy(s2_ref.at[r], out_ref.at[r], row_sems.at[r])

        def send(r, c):
            copy(r).start()
            return c

        def wait(r, c):
            copy(r).wait()
            return c

        lax.fori_loop(head, jnp.minimum(begin, tail), send, 0)
        lax.fori_loop(end, tail, send, 0)

        @pl.when(trim[2] > 0)
        def _():
            res = (bef + first_ref[...].astype(F32)).astype(BF16)
            add_fix(inv_ref[trim[4]], res, s2_ref, 0, head)
            lax.fori_loop(0, head, send, 0)

        @pl.when(trim[3] > 0)
        def _():
            res = (last_ref[...].astype(F32) + aft).astype(BF16)
            add_fix(inv_ref[trim[5]], res, s2_ref, tail, p.R)
            lax.fori_loop(tail, p.R, send, 0)

        lax.fori_loop(0, begin, wait, 0)
        lax.fori_loop(end, p.R, wait, 0)

    return pl.pallas_call(
        kernel,
        in_specs=[SMEM] * 3 + [VM] * 6 + [HBM],
        out_specs=[VM, HBM],
        out_shape=[
            pltpu.VMEM((p.R, p.BS, p.N), F32),
            jax.ShapeDtypeStruct((p.R, p.BS, p.N), F32),
        ],
        input_output_aliases={7: 0, 9: 1},
        scratch_shapes=[pltpu.SemaphoreType.DMA((p.R,))],
        compiler_params=params(8),
        cost_estimate=cost(4 * p.BS * p.BS * p.N, p.R * p.BS * p.N),
        name="coarse_split",
    )(
        pos, bounds, trims, near(part_first), near(part_last), *map(near, parts), near(s2), near(inv), out
    )[1]


def swaps(axis, odd):
    size = lax.axis_size(axis)
    pairs = [(i, i + 1) for i in range(odd, size - 1, 2)]
    return lambda value: lax.ppermute(value, axis, pairs + [(j, i) for i, j in pairs])


def body(load_rhs, blocks, columns, counts, smoother, agg_sizes, coarse_inv):
    rows, bs, n = load_rhs.shape
    group = lax.axis_size("agg")
    p = Sizes(rows, blocks.shape[1], bs, n, agg_sizes.shape[1], group)
    here = lax.axis_index("agg")
    index = lax.axis_index(AXES)
    pos = jnp.stack([index * rows, here, index & 1]).astype(I32)

    swap_odd, swap_even = swaps(AXES, 1), swaps(AXES, 0)

    out1 = edge_smooth(p, pos, load_rhs, smoother)
    inner1 = swap_odd(out1[0]), swap_even(out1[1])
    outer1 = swap_odd(out1[2]), swap_even(out1[3])

    def every(own):
        turn = lambda t: lax.ppermute(own, "agg", [(i, (i + t) % group) for i in range(group)])
        return jnp.stack([turn(t) for t in range(1, group)])

    def none(own):
        return jnp.zeros((group - 1,) + own.shape, own.dtype)

    sizes, _ = lax.optimization_barrier((agg_sizes, out1[0]))
    ids = jnp.arange(p.A, dtype=I32)
    ends = jnp.sum(jnp.where(ids[None, :] <= ids[:, None], sizes, 0), axis=1)
    owner = ids // (p.A // group)
    reach = jnp.maximum((ends - 1) // rows - owner, owner - (ends - sizes[0]) // rows)
    apart = jnp.max(reach)[None]
    distant = lax.cond(apart[0] > 1, every, none, coarse_inv)
    inverses = coarse_inv, swaps("agg", 1)(coarse_inv), swaps("agg", 0)(coarse_inv), distant
    rhs, smoother, end_blocks, inv, s2, ext1, acc1, lcol, hslot, hcol, hn, bounds, trims = first_sweep(
        p, pos, columns.T, counts[None, :], agg_sizes, load_rhs, smoother, blocks, apart, inverses
    )
    acc1, s2, ext2, halo, *out2 = edge_second(
        p, False, pos, hslot, hcol, hn, inner1, acc1, smoother, end_blocks, s2
    )
    inner2 = swap_odd(out2[0]), swap_even(out2[1])
    acc1 = outer_local(p, lcol, rhs, end_blocks, ext1, acc1)
    _, s2, ext2, _, *out2 = edge_second(
        p, True, pos, hslot, hcol, hn, outer1, acc1, smoother, end_blocks, s2, ext2, halo
    )
    outer2 = swap_odd(out2[0]), swap_even(out2[1])
    ext2, s2, inner_blocks = inner_second(p, lcol, rhs, smoother, ext1, ext2, s2, blocks)
    r2, acc2, s2, halo, out = inner_rows(
        p, pos, lcol, bounds, rhs, end_blocks, inner_blocks, ext2, s2, inner2, inv
    )
    r2, _, _, part_first, part_last, to_odd, to_even = edge_final(
        p, pos, hslot, hcol, hn, trims, outer2, halo, acc2, end_blocks, r2
    )
    parts = swaps("agg", 1)(to_odd), swaps("agg", 0)(to_even)
    s2 = coarse_own(p, bounds, trims, r2, s2, inv)
    return coarse_split(p, pos, bounds, trims, part_first, part_last, parts, s2, inv, out)


def solution(mesh):
    placed = (
        P(AXES, None, None),
        P(AXES, None, None, None),
        P(AXES, None),
        P(AXES),
        P(AXES, None, None),
        P("rows", None),
        P(AXES, None, None),
    )
    return jax.shard_map(
        body, mesh=mesh, in_specs=placed, out_specs=P(AXES, None, None), check_vma=False
    )
```

```python
import jax
import jax.numpy as jnp
from jax import lax
from jax.experimental import pallas as pl
from jax.experimental.pallas import tpu as pltpu
from jax.sharding import PartitionSpec as P

HALO = 16

relax_fine = 0.8
relax_coarse = 1.0

AXES = ("rows", "agg")
F32 = jnp.float32
BF16 = jnp.bfloat16
I32 = jnp.int32
MIB = 1024 * 1024
WEIGHT = 32

SMEM = pl.BlockSpec(memory_space=pltpu.SMEM)
VM = pl.BlockSpec(memory_space=pltpu.VMEM)
ANY = pl.BlockSpec(memory_space=pl.ANY)
HBM = pl.BlockSpec(memory_space=pltpu.HBM)


def mm(a, b):
    return jnp.dot(a, b, preferred_element_type=F32)


def cost(flops, nbytes):
    return pl.CostEstimate(flops=WEIGHT * flops, bytes_accessed=nbytes, transcendentals=0)


def params(mib):
    return pltpu.CompilerParams(vmem_limit_bytes=mib * MIB)


def near(x):
    return pltpu.with_memory_space_constraint(x, pltpu.VMEM)


def far(x):
    return pltpu.with_memory_space_constraint(x, pltpu.HBM)


class Sizes:
    def __init__(self, rows, slots, bs, n, aggs, group):
        self.R, self.K, self.BS, self.N, self.A, self.G = rows, slots, bs, n, aggs, group
        self.H = HALO


def edge_smooth(p, pos, rhs, smoother):
    step = p.H // 2

    def kernel(pos_ref, b_hbm, s_hbm, *rest):
        outs, (b, s, sems) = rest[:4], rest[4:]
        odd = pos_ref[2]
        starts = []
        for first, last in ((0, p.R - step), (step, p.R - 2 * step)):
            starts += [jnp.where(odd > 0, last, first), jnp.where(odd > 0, first, last)]
        copies = []
        for c, at in enumerate(starts):
            copies.append(pltpu.make_async_copy(b_hbm.at[pl.ds(at, step)], b.at[c], sems.at[0, c]))
            copies.append(pltpu.make_async_copy(s_hbm.at[pl.ds(at, step)], s.at[c], sems.at[1, c]))
        for c in copies:
            c.start()

        for c in range(4):
            copies[2 * c].wait()
            copies[2 * c + 1].wait()
            for r in range(step):
                outs[c][r] = (relax_fine * mm(s[c, r], b[c, r])).astype(BF16)

    out = jax.ShapeDtypeStruct((step, p.BS, p.N), BF16)
    return pl.pallas_call(
        kernel,
        in_specs=[SMEM, HBM, HBM],
        out_specs=[VM] * 4,
        out_shape=[out] * 4,
        scratch_shapes=[
            pltpu.VMEM((4, step, p.BS, p.N), BF16),
            pltpu.VMEM((4, step, p.BS, p.BS), BF16),
            pltpu.SemaphoreType.DMA((2, 4)),
        ],
        compiler_params=params(8),
        cost_estimate=cost(4 * p.H * p.BS * p.BS * p.N, 6 * p.H * p.BS * p.N),
        name="edge_smooth",
    )(pos, far(rhs), far(smoother))


def end_row(p, r):
    return jnp.where(r < p.H, r, r + p.R - 2 * p.H)


def row_product(p, blk, at, i, ext, lcol):
    lhs = jnp.concatenate([blk[at, k] for k in range(p.K)], axis=1)
    rhs = jnp.concatenate([ext[lcol[k, i]] for k in range(p.K)], axis=0)
    return mm(lhs, rhs)


def first_sweep(p, pos, cols, counts, sizes, rhs, smoother, blocks, apart, inverses):
    piece = p.H // 2
    share = p.A // p.G
    pieces = p.R // piece
    end_pieces = 2 * p.H // piece

    def kernel(
        pos_ref, col_ref, cnt_ref, size_ref, b_hbm, sm_hbm, blk_hbm, apart_ref, own, by_odd, by_even, distant,
        b, sm, blk, inv, s2, ext, acc, lcol, hslot, hcol, hn, bounds, trims, lists, sems, list_sems, inv_sems,
    ):
        start, here = pos_ref[0], pos_ref[1]
        small = [
            pltpu.make_async_copy(src.at[pl.ds(c * piece, piece)], dst.at[pl.ds(c * piece, piece)], sems.at[j, c])
            for c in range(pieces)
            for j, (src, dst) in enumerate(((b_hbm, b), (sm_hbm, sm)))
        ]

        def block_copy(c):
            src = pl.ds(c * piece if c < end_pieces // 2 else p.R - 2 * p.H + c * piece, piece)
            return pltpu.make_async_copy(blk_hbm.at[src], blk.at[pl.ds(c * piece, piece)], sems.at[2, c])

        for c in small:
            c.start()
        for c in range(end_pieces):
            block_copy(c).start()
        back = jnp.where((pos_ref[1] & 1) > 0, p.G - 1, 1)

        def inverse_copy(src, distance, t):
            at = pl.ds(lax.rem(pos_ref[1] - distance + p.G, p.G) * share, share)
            return pltpu.make_async_copy(src, inv.at[at], inv_sems.at[t])

        def place_all(act):
            act(inverse_copy(own, 0, 0))

            @pl.when(apart_ref[0] <= 1)
            def _():
                act(inverse_copy(by_odd, back, 1))
                act(inverse_copy(by_even, p.G - back, 2))

            @pl.when(apart_ref[0] > 1)
            def _():
                for t in range(1, p.G):
                    act(inverse_copy(distant.at[t - 1], t, t))

        place_all(lambda c: c.start())
        ext[p.R] = jnp.zeros((p.BS, p.N), BF16)

        cols = col_ref[...] - start
        ks = lax.broadcasted_iota(I32, (p.K, p.R), 0)
        live = ks < cnt_ref[...]
        inside = jnp.logical_and(cols >= 0, cols < p.R)
        lists[0] = jnp.where(jnp.logical_and(live, inside), cols, p.R)
        outside = jnp.where(jnp.logical_and(live, jnp.logical_not(inside)), 1, 0)
        place = jnp.where(cols < 0, cols + p.H, cols - p.R + p.H)
        count = jnp.zeros((1, p.R), I32)
        slot_rows = [jnp.zeros((1, p.R), I32)] * p.K
        col_rows = [jnp.full((1, p.R), 2 * p.H, I32)] * p.K
        for k in range(p.K):
            out = outside[k:k + 1]
            for j in range(k + 1):
                mine = jnp.logical_and(out > 0, count == j)
                slot_rows[j] = jnp.where(mine, k, slot_rows[j])
                col_rows[j] = jnp.where(mine, place[k:k + 1], col_rows[j])
            count = count + out
        lists[1] = jnp.concatenate(slot_rows, axis=0)
        lists[2] = jnp.concatenate(col_rows, axis=0)
        lists[3] = jnp.broadcast_to(count, (p.K, p.R))
        list_copies = [
            pltpu.make_async_copy(lists.at[j], dst, list_sems.at[j]) for j, dst in enumerate((lcol, hslot, hcol, hn))
        ]
        for c in list_copies:
            c.start()

        def smooth_row(r, c):
            v = relax_fine * mm(sm[r], b[r])
            s2[r] = v
            ext[r] = v.astype(BF16)
            return c

        for c in range(pieces):
            small[2 * c].wait()
            small[2 * c + 1].wait()
            lax.fori_loop(c * piece, (c + 1) * piece, smooth_row, 0, unroll=8)

        for c in list_copies:
            c.wait()

        def edge_row(r, c):
            i = end_row(p, r)
            acc[r] = b[i].astype(F32) - row_product(p, blk, r, i, ext, lcol)
            return c

        for c in range(end_pieces):
            block_copy(c).wait()
            if c not in (0, end_pieces - 1):
                lax.fori_loop(c * piece, (c + 1) * piece, edge_row, 0, unroll=8)

        place_all(lambda c: c.wait())

        bounds[0] = 0

        def agg(a, t):
            end, first, last, before, after, lowest, highest = t
            begin = end
            end = end + size_ref[0, a]
            bounds[a + 1] = jnp.clip(end, 0, p.R)
            leads = jnp.logical_and(begin <= 0, end > 0)
            ends = jnp.logical_and(begin < p.R, end >= p.R)
            first = jnp.where(leads, end, first)
            last = jnp.where(ends, begin, last)
            lowest = jnp.where(leads, a, lowest)
            highest = jnp.where(ends, a, highest)
            before = jnp.where(jnp.logical_and(begin < 0, end > 0), 1, before)
            after = jnp.where(jnp.logical_and(begin < p.R, end > p.R), 1, after)
            return end, first, last, before, after, lowest, highest

        zero = jnp.int32(0)
        _, first, last, before, after, lowest, highest = lax.fori_loop(0, p.A, agg, (-here * p.R,) + (zero,) * 6)
        trims[0] = jnp.clip(first, 0, p.R)
        trims[1] = jnp.clip(last, 0, p.R)
        trims[2] = before
        trims[3] = after
        trims[4] = lowest
        trims[5] = highest

    ints = lambda n: jax.ShapeDtypeStruct((n,), I32)
    return pl.pallas_call(
        kernel,
        in_specs=[SMEM, VM, VM, SMEM] + [HBM] * 3 + [SMEM] + [ANY] * 4,
        out_specs=[VM] * 7 + [SMEM] * 6,
        out_shape=[
            pltpu.VMEM(rhs.shape, BF16),
            pltpu.VMEM(smoother.shape, BF16),
            pltpu.VMEM((2 * p.H,) + blocks.shape[1:], BF16),
            pltpu.VMEM((p.A, p.BS, p.BS), BF16),
            pltpu.VMEM((p.R, p.BS, p.N), F32),
            pltpu.VMEM((p.R + 1, p.BS, p.N), BF16),
            pltpu.VMEM((2 * p.H, p.BS, p.N), F32),
            *[jax.ShapeDtypeStruct((p.K, p.R), I32)] * 4,
            ints(p.A + 1),
            ints(6),
        ],
        scratch_shapes=[
            pltpu.VMEM((4, p.K, p.R), I32),
            pltpu.SemaphoreType.DMA((3, pieces)),
            pltpu.SemaphoreType.DMA((4,)),
            pltpu.SemaphoreType.DMA((p.G,)),
        ],
        compiler_params=params(8),
        cost_estimate=cost(2 * p.R * p.K * p.BS * p.BS * p.N, 2 * p.R * p.K * p.BS * p.BS),
        name="first_sweep",
    )(pos, cols, counts, sizes, far(rhs), far(smoother), far(blocks), apart, *inverses)


GROUP = 4
NARROW, WIDE = 4, 6


def outer_local(p, lcol, rhs, blocks, ext, acc):
    step = p.H // 2

    def kernel(lcol_ref, b, blk, ext_ref, acc_in, acc_ref):
        def edge_row(r, c):
            i = end_row(p, r)
            acc_ref[r] = b[i].astype(F32) - row_product(p, blk, r, i, ext_ref, lcol_ref)
            return c

        lax.fori_loop(0, step, edge_row, 0, unroll=8)
        lax.fori_loop(2 * p.H - step, 2 * p.H, edge_row, 0, unroll=8)

    return pl.pallas_call(
        kernel,
        in_specs=[SMEM] + [VM] * 4,
        out_specs=VM,
        out_shape=pltpu.VMEM((2 * p.H, p.BS, p.N), F32),
        input_output_aliases={4: 0},
        compiler_params=params(8),
        cost_estimate=cost(0, 0),
        name="outer_local",
    )(lcol, near(rhs), near(blocks), near(ext), near(acc))


def halo_product(hslot, hcol, blk, r, i, slots, halo):
    lhs = jnp.concatenate([blk[r, hslot[j, i]] for j in slots], axis=1)
    rhs = jnp.concatenate([halo[hcol[j, i]] for j in slots], axis=0)
    return mm(lhs, rhs)


def take_rest(p, hslot, hcol, hn, blk, halo, acc, rows, taken):
    def row(r, c):
        i = end_row(p, r)

        @pl.when(hn[0, i] > taken)
        def _():
            acc[r] = acc[r] - halo_product(hslot, hcol, blk, r, i, range(taken, p.K), halo)

        return c

    for first, last in rows:
        lax.fori_loop(first, last, row, 0)


def put_halo(p, odd, halo, from_odd, from_even, before, after):
    step = p.H // 2
    halo[pl.ds(jnp.where(odd > 0, after, before), step)] = from_odd[...]
    halo[pl.ds(jnp.where(odd > 0, before, after), step)] = from_even[...]


def edge_second(p, outer, pos, hslot, hcol, hn, parts, acc, smoother, blocks, s2, ext2=None, halo=None):
    step = p.H // 2
    halves = ((0, step), (2 * p.H - step, 2 * p.H)) if outer else ((step, p.H), (p.H, p.H + step))
    before, after = (0, 2 * p.H - step) if outer else (step, p.H)
    taken = min(p.K, WIDE if outer else NARROW)

    def kernel(pos_ref, hs, hc, hn_ref, acc_in, s2_in, *rest):
        from_odd, from_even, sm, blk = rest[-12:-8]
        acc_ref, s2_out, ext_out, halo_ref, to_odd, to_even, res, sent = rest[-8:]
        odd = pos_ref[2]
        put_halo(p, odd, halo_ref, from_odd, from_even, before, after)
        if not outer:
            halo_ref[2 * p.H] = jnp.zeros((p.BS, p.N), BF16)
            ext_out[p.R] = jnp.zeros((p.BS, p.N), BF16)
        take_rest(p, hs, hc, hn_ref, blk, halo_ref, acc_ref, halves, taken)
        for first, last in halves:

            def residual(r, c):
                i = end_row(p, r)
                res[r] = (acc_ref[r] - halo_product(hs, hc, blk, r, i, range(taken), halo_ref)).astype(BF16)
                return c

            lax.fori_loop(first, last, residual, 0, unroll=8)
        for h, (first, last) in enumerate(halves):
            shift_by = 0 if first < p.H else p.R - 2 * p.H
            for g in range(first, last, GROUP):
                rows = range(g, g + GROUP)
                new = [s2_in[shift_by + r] + relax_fine * mm(sm[shift_by + r], res[r]) for r in rows]
                for r, v in zip(rows, new):
                    s2_out[shift_by + r] = v
                    sent[h, r - first] = v.astype(BF16)
                    ext_out[shift_by + r] = v.astype(BF16)
        to_odd[...] = sent[odd]
        to_even[...] = sent[1 - odd]

    out = jax.ShapeDtypeStruct((step, p.BS, p.N), BF16)
    kept = [] if not outer else [near(ext2), near(halo)]
    return pl.pallas_call(
        kernel,
        in_specs=[SMEM] * 4 + [VM] * (6 + len(kept)),
        out_specs=[VM] * 6,
        out_shape=[
            pltpu.VMEM((2 * p.H, p.BS, p.N), F32),
            pltpu.VMEM((p.R, p.BS, p.N), F32),
            pltpu.VMEM((p.R + 1, p.BS, p.N), BF16),
            pltpu.VMEM((2 * p.H + 1, p.BS, p.N), BF16),
            out,
            out,
        ],
        input_output_aliases={4: 0, 5: 1, **({6: 2, 7: 3} if outer else {})},
        scratch_shapes=[
            pltpu.VMEM((2 * p.H, p.BS, p.N), BF16),
            pltpu.VMEM((2, step, p.BS, p.N), BF16),
        ],
        compiler_params=params(8),
        cost_estimate=cost(8 * p.H * p.BS * p.BS * p.N, 4 * p.H * p.K * p.BS * p.BS),
        name="edge_second_outer" if outer else "edge_second_inner",
    )(
        pos, hslot, hcol, hn, near(acc), near(s2), *kept, near(parts[0]), near(parts[1]), near(smoother), near(blocks)
    )


def aggregate_sum(p, resid, first, last):
    return lax.fori_loop(
        first, last, lambda r, t: t + resid[r].astype(F32), jnp.zeros((p.BS, p.N), F32)
    )


def add_fix(inverse, res, s2, first, last):
    fix = (relax_coarse * mm(inverse, res)).astype(BF16).astype(F32)

    def row(r, c):
        s2[r] = s2[r] + fix
        return c

    lax.fori_loop(first, last, row, 0)


def inner_aggregate(p, first, last):
    return jnp.logical_and(first >= p.H, last <= p.R - p.H)


def inner_second(p, lcol, rhs, smoother, ext1, ext2, s2, blocks):
    piece = 8
    inner = p.R - 2 * p.H

    def kernel(lcol_ref, b, sm, ext1_ref, ext_in, s2_ref, blk_hbm, ext, s2_out, blk, blk_sems):
        def block_copy(c):
            src = blk_hbm.at[pl.ds(p.H + c * piece, piece)]
            return pltpu.make_async_copy(src, blk.at[pl.ds(c * piece, piece)], blk_sems.at[c])

        for c in range(inner // piece):
            block_copy(c).start()
        for c in range(inner // piece):
            block_copy(c).wait()
            rows = range(c * piece, (c + 1) * piece)
            res = [
                (b[p.H + r].astype(F32) - row_product(p, blk, r, p.H + r, ext1_ref, lcol_ref)).astype(BF16) for r in rows
            ]
            new = [s2_ref[p.H + r] + relax_fine * mm(sm[p.H + r], v) for r, v in zip(rows, res)]
            for r, v in zip(rows, new):
                s2_out[p.H + r] = v
                ext[p.H + r] = v.astype(BF16)

    return pl.pallas_call(
        kernel,
        in_specs=[SMEM] + [VM] * 5 + [HBM],
        out_specs=[VM] * 3,
        out_shape=[
            pltpu.VMEM((p.R + 1, p.BS, p.N), BF16),
            pltpu.VMEM((p.R, p.BS, p.N), F32),
            pltpu.VMEM((inner,) + blocks.shape[1:], BF16),
        ],
        input_output_aliases={4: 0, 5: 1},
        scratch_shapes=[pltpu.SemaphoreType.DMA((inner // piece,))],
        compiler_params=params(8),
        cost_estimate=cost(0, 0),
        name="inner_second",
    )(lcol, near(rhs), near(smoother), near(ext1), near(ext2), near(s2), far(blocks))


def inner_rows(p, pos, lcol, bounds, rhs, end_blocks, blocks, ext, s2, parts, inv):
    inner = p.R - 2 * p.H

    def kernel(
        pos_ref, lcol_ref, bd, b, end_blk, blk, ext, inv, s2_ref, from_odd, from_even,
        r2, acc, s2_out, halo, out, row_sems,
    ):
        put_halo(p, pos_ref[2], halo, from_odd, from_even, 0, 2 * p.H - p.H // 2)

        def inner_row(r, c):
            i = p.H + r
            r2[i] = (b[i].astype(F32) - row_product(p, blk, r, i, ext, lcol_ref)).astype(BF16)
            return c

        lax.fori_loop(0, inner, inner_row, 0, unroll=16)

        def copy(r):
            return pltpu.make_async_copy(s2_out.at[r], out.at[r], row_sems.at[r])

        def send(r, c):
            copy(r).start()
            return c

        def wait(r, c):
            copy(r).wait()
            return c

        def aggregates(act):
            def one(a, c):
                first, last = bd[a], bd[a + 1]
                pl.when(jnp.logical_and(first < last, inner_aggregate(p, first, last)))(lambda: act(a, first, last))
                return c

            lax.fori_loop(0, p.A, one, 0)

        def fix(a, first, last):
            res = aggregate_sum(p, r2, first, last).astype(BF16)
            add_fix(inv[a], res, s2_out, first, last)
            lax.fori_loop(first, last, send, 0)

        aggregates(fix)

        def edge_row(r, c):
            i = end_row(p, r)
            acc[r] = b[i].astype(F32) - row_product(p, end_blk, r, i, ext, lcol_ref)
            return c

        lax.fori_loop(0, 2 * p.H, edge_row, 0, unroll=16)

        def settle(a, first, last):
            lax.fori_loop(first, last, wait, 0)

        aggregates(settle)

    return pl.pallas_call(
        kernel,
        in_specs=[SMEM] * 3 + [VM] * 8,
        out_specs=[VM] * 4 + [HBM],
        out_shape=[
            pltpu.VMEM((p.R, p.BS, p.N), BF16),
            pltpu.VMEM((2 * p.H, p.BS, p.N), F32),
            pltpu.VMEM((p.R, p.BS, p.N), F32),
            pltpu.VMEM((2 * p.H + 1, p.BS, p.N), BF16),
            jax.ShapeDtypeStruct((p.R, p.BS, p.N), F32),
        ],
        input_output_aliases={8: 2},
        scratch_shapes=[pltpu.SemaphoreType.DMA((p.R,))],
        compiler_params=params(8),
        cost_estimate=cost(4 * p.R * p.K * p.BS * p.BS * p.N, p.R * p.K * p.BS * p.BS),
        name="inner_rows",
    )(
        pos, lcol, bounds, near(rhs), near(end_blocks), near(blocks), near(ext), near(inv), near(s2), *map(near, parts)
    )


def edge_final(p, pos, hslot, hcol, hn, trims, parts, halo, acc, blocks, r2):
    step = p.H // 2

    def kernel(pos_ref, hs, hc, hn_ref, trim, from_odd, from_even, halo_in, acc_in, blk, r2_in, *rest):
        r2_out, acc_ref, halo, part_first, part_last, to_odd, to_even, both = rest
        put_halo(p, pos_ref[2], halo, from_odd, from_even, step, p.H)
        halo[2 * p.H] = jnp.zeros((p.BS, p.N), BF16)
        inner = ((step, 2 * p.H - step),)
        outer = ((0, step), (2 * p.H - step, 2 * p.H))
        for rows, taken in ((inner, min(p.K, NARROW)), (outer, min(p.K, WIDE))):
            take_rest(p, hs, hc, hn_ref, blk, halo, acc_ref, rows, taken)
            for first, last in rows:

                def row(r, c):
                    i = end_row(p, r)
                    r2_out[i] = (acc_ref[r] - halo_product(hs, hc, blk, r, i, range(taken), halo)).astype(BF16)
                    return c

                lax.fori_loop(first, last, row, 0, unroll=8)
        both[0] = aggregate_sum(p, r2_out, 0, trim[0]).astype(BF16)
        both[1] = aggregate_sum(p, r2_out, trim[1], p.R).astype(BF16)
        part_first[...] = both[0]
        part_last[...] = both[1]
        odd = pos_ref[1] & 1
        to_odd[...] = both[odd]
        to_even[...] = both[1 - odd]

    one = jax.ShapeDtypeStruct((p.BS, p.N), BF16)
    return pl.pallas_call(
        kernel,
        in_specs=[SMEM] * 5 + [VM] * 6,
        out_specs=[VM] * 7,
        out_shape=[
            pltpu.VMEM((p.R, p.BS, p.N), BF16),
            pltpu.VMEM((2 * p.H, p.BS, p.N), F32),
            pltpu.VMEM((2 * p.H + 1, p.BS, p.N), BF16),
            *[one] * 4,
        ],
        input_output_aliases={10: 0, 8: 1, 7: 2},
        scratch_shapes=[pltpu.VMEM((2, p.BS, p.N), BF16)],
        compiler_params=params(8),
        cost_estimate=cost(4 * p.H * p.BS * p.BS * p.N, 4 * p.H * p.K * p.BS * p.BS),
        name="edge_final",
    )(pos, hslot, hcol, hn, trims, *map(near, parts), near(halo), near(acc), near(blocks), near(r2))


def coarse_own(p, bounds, trims, r2, s2, inv):
    def kernel(bd, trim, r2_ref, s2_in, inv_ref, s2_ref):
        def one(a, c):
            first, last = bd[a], bd[a + 1]
            split = jnp.logical_or(
                jnp.logical_and(first == 0, trim[2] > 0), jnp.logical_and(last == p.R, trim[3] > 0)
            )
            done = jnp.logical_or(split, inner_aggregate(p, first, last))

            @pl.when(jnp.logical_and(first < last, jnp.logical_not(done)))
            def _():
                res = aggregate_sum(p, r2_ref, first, last).astype(BF16)
                add_fix(inv_ref[a], res, s2_ref, first, last)

            return c

        lax.fori_loop(0, p.A, one, 0)

    return pl.pallas_call(
        kernel,
        in_specs=[SMEM] * 2 + [VM] * 3,
        out_specs=VM,
        out_shape=pltpu.VMEM((p.R, p.BS, p.N), F32),
        input_output_aliases={3: 0},
        compiler_params=params(8),
        cost_estimate=cost(p.A * p.BS * p.BS * p.N, 5 * p.R * p.BS * p.N),
        name="coarse_own",
    )(bounds, trims, near(r2), near(s2), near(inv))


def coarse_split(p, pos, bounds, trims, part_first, part_last, parts, s2, inv, out):
    def kernel(
        pos_ref, bd, trim, first_ref, last_ref, by_odd, by_even, s2_in, inv_ref, out_in, s2_ref, out_ref, row_sems
    ):
        odd = (pos_ref[1] & 1) > 0
        bef = jnp.where(odd, by_even[...].astype(F32), by_odd[...].astype(F32))
        aft = jnp.where(odd, by_odd[...].astype(F32), by_even[...].astype(F32))

        def inner(a, t):
            begin, end = t
            first, last = bd[a], bd[a + 1]
            sent = jnp.logical_and(first < last, inner_aggregate(p, first, last))
            return jnp.where(sent, jnp.minimum(begin, first), begin), jnp.where(sent, last, end)

        begin, end = lax.fori_loop(0, p.A, inner, (jnp.int32(p.R), jnp.int32(p.R)))
        head = jnp.where(trim[2] > 0, trim[0], 0)
        tail = jnp.where(trim[3] > 0, trim[1], p.R)

        def copy(r):
            return pltpu.make_async_copy(s2_ref.at[r], out_ref.at[r], row_sems.at[r])

        def send(r, c):
            copy(r).start()
            return c

        def wait(r, c):
            copy(r).wait()
            return c

        lax.fori_loop(head, jnp.minimum(begin, tail), send, 0)
        lax.fori_loop(end, tail, send, 0)

        @pl.when(trim[2] > 0)
        def _():
            res = (bef + first_ref[...].astype(F32)).astype(BF16)
            add_fix(inv_ref[trim[4]], res, s2_ref, 0, head)
            lax.fori_loop(0, head, send, 0)

        @pl.when(trim[3] > 0)
        def _():
            res = (last_ref[...].astype(F32) + aft).astype(BF16)
            add_fix(inv_ref[trim[5]], res, s2_ref, tail, p.R)
            lax.fori_loop(tail, p.R, send, 0)

        lax.fori_loop(0, begin, wait, 0)
        lax.fori_loop(end, p.R, wait, 0)

    return pl.pallas_call(
        kernel,
        in_specs=[SMEM] * 3 + [VM] * 6 + [HBM],
        out_specs=[VM, HBM],
        out_shape=[
            pltpu.VMEM((p.R, p.BS, p.N), F32),
            jax.ShapeDtypeStruct((p.R, p.BS, p.N), F32),
        ],
        input_output_aliases={7: 0, 9: 1},
        scratch_shapes=[pltpu.SemaphoreType.DMA((p.R,))],
        compiler_params=params(8),
        cost_estimate=cost(4 * p.BS * p.BS * p.N, p.R * p.BS * p.N),
        name="coarse_split",
    )(
        pos, bounds, trims, near(part_first), near(part_last), *map(near, parts), near(s2), near(inv), out
    )[1]


def swaps(axis, odd):
    size = lax.axis_size(axis)
    pairs = [(i, i + 1) for i in range(odd, size - 1, 2)]
    return lambda value: lax.ppermute(value, axis, pairs + [(j, i) for i, j in pairs])


def body(load_rhs, blocks, columns, counts, smoother, agg_sizes, coarse_inv):
    rows, bs, n = load_rhs.shape
    group = lax.axis_size("agg")
    p = Sizes(rows, blocks.shape[1], bs, n, agg_sizes.shape[1], group)
    here = lax.axis_index("agg")
    index = lax.axis_index(AXES)
    pos = jnp.stack([index * rows, here, index & 1]).astype(I32)

    swap_odd, swap_even = swaps(AXES, 1), swaps(AXES, 0)

    out1 = edge_smooth(p, pos, load_rhs, smoother)
    inner1 = swap_odd(out1[0]), swap_even(out1[1])
    outer1 = swap_odd(out1[2]), swap_even(out1[3])

    def every(own):
        turn = lambda t: lax.ppermute(own, "agg", [(i, (i + t) % group) for i in range(group)])
        return jnp.stack([turn(t) for t in range(1, group)])

    def none(own):
        return jnp.zeros((group - 1,) + own.shape, own.dtype)

    sizes, _ = lax.optimization_barrier((agg_sizes, out1[0]))
    ids = jnp.arange(p.A, dtype=I32)
    ends = jnp.sum(jnp.where(ids[None, :] <= ids[:, None], sizes, 0), axis=1)
    owner = ids // (p.A // group)
    reach = jnp.maximum((ends - 1) // rows - owner, owner - (ends - sizes[0]) // rows)
    apart = jnp.max(reach)[None]
    distant = lax.cond(apart[0] > 1, every, none, coarse_inv)
    inverses = coarse_inv, swaps("agg", 1)(coarse_inv), swaps("agg", 0)(coarse_inv), distant
    rhs, smoother, end_blocks, inv, s2, ext1, acc1, lcol, hslot, hcol, hn, bounds, trims = first_sweep(
        p, pos, columns.T, counts[None, :], agg_sizes, load_rhs, smoother, blocks, apart, inverses
    )
    acc1, s2, ext2, halo, *out2 = edge_second(
        p, False, pos, hslot, hcol, hn, inner1, acc1, smoother, end_blocks, s2
    )
    inner2 = swap_odd(out2[0]), swap_even(out2[1])
    acc1 = outer_local(p, lcol, rhs, end_blocks, ext1, acc1)
    _, s2, ext2, _, *out2 = edge_second(
        p, True, pos, hslot, hcol, hn, outer1, acc1, smoother, end_blocks, s2, ext2, halo
    )
    outer2 = swap_odd(out2[0]), swap_even(out2[1])
    ext2, s2, inner_blocks = inner_second(p, lcol, rhs, smoother, ext1, ext2, s2, blocks)
    r2, acc2, s2, halo, out = inner_rows(
        p, pos, lcol, bounds, rhs, end_blocks, inner_blocks, ext2, s2, inner2, inv
    )
    r2, _, _, part_first, part_last, to_odd, to_even = edge_final(
        p, pos, hslot, hcol, hn, trims, outer2, halo, acc2, end_blocks, r2
    )
    parts = swaps("agg", 1)(to_odd), swaps("agg", 0)(to_even)
    s2 = coarse_own(p, bounds, trims, r2, s2, inv)
    return coarse_split(p, pos, bounds, trims, part_first, part_last, parts, s2, inv, out)


def solution(mesh):
    placed = (
        P(AXES, None, None),
        P(AXES, None, None, None),
        P(AXES, None),
        P(AXES),
        P(AXES, None, None),
        P("rows", None),
        P(AXES, None, None),
    )
    return jax.shard_map(
        body, mesh=mesh, in_specs=placed, out_specs=P(AXES, None, None), check_vma=False
    )
```
